512 devices in a mesh: rows: 128 (over x, y, z_hi, core), ch: 4 (over z_lo).
Axes of the slice: x: 4, y: 4, z: 16 (z_hi: 4, z_lo: 4; z = z_hi * 4 + z_lo), core: 2. Of those that a mesh axis runs over, the one named last changes fastest.
Arguments:
- pixels: bfloat16 [256, 1024, 256], P('ch', 'rows'), may hold values from -24 to 24
- conv_gain: float32 [256], replicated, may hold values from 0.25 to 1.75
- expand_weight: bfloat16 [256, 1024], replicated, may hold values from -0.375 to 0.375
- depth_kernel: bfloat16 [3, 3, 1024], replicated, may hold values from -2 to 2
- shrink_weight: bfloat16 [1024, 256], replicated, may hold values from -0.1875 to 0.1875
- block_gain: float32 [256], replicated, may hold values from 0.25 to 1.75
- block_qkv: bfloat16 [256, 768], replicated, may hold values from -0.375 to 0.375
- block_merge: bfloat16 [256, 256], replicated, may hold values from -0.375 to 0.375
- block_bias: float32 [8, 15, 15], replicated, may hold values from -3 to 400
- grid_gain: float32 [256], replicated, may hold values from 0.25 to 1.75
- grid_qkv: bfloat16 [256, 768], replicated, may hold values from -0.375 to 0.375
- grid_merge: bfloat16 [256, 256], replicated, may hold values from -0.375 to 0.375
- grid_bias: float32 [8, 15, 15], replicated, may hold values from -3 to 400
- mlp_gain: float32 [256], replicated, may hold values from 0.25 to 1.75
- mlp_up: bfloat16 [256, 1024], replicated, may hold values from -0.375 to 0.375
- mlp_down: bfloat16 [1024, 256], replicated, may hold values from -0.1875 to 0.1875
Outputs:
- block_output: bfloat16 [256, 1024, 256], P('ch', 'rows')
The draws below stay inside these ranges and needn't reach their ends.
All inputs are finite; a program needn't handle non-finite values.
Results may differ from the reference program's by a relative error of at most 0.02.
Values may be sent and summed in bfloat16 or wider, within the bound.
A program may use at most 64 MiB of HBM per device.

```python
import math
import jax
import jax.numpy as jnp
from jax import lax

C = 256
HEADS = 8
HEAD_DIM = 32
HID = 1024
WIN = 8
BAND = 8
W = 256
H = 1024


def draw_pixels(key, part):
    noise_key, chan_key, place_key = jax.random.split(key, 3)
    noise = jax.random.truncated_normal(noise_key, -3.0, 3.0, (C, H, W), jnp.float32)
    chan_scale = jnp.exp(jax.random.uniform(chan_key, (C, 1, 1), jnp.float32, math.log(0.5), math.log(2.0)))
    place_scale = jnp.exp(jax.random.uniform(place_key, (1, H, W), jnp.float32, math.log(0.5), math.log(2.0)))
    return (noise * chan_scale * place_scale).astype(jnp.bfloat16)


def relative_table(key):
    offset_table = jax.random.truncated_normal(key, -3.0, 3.0, (HEADS, 2 * WIN - 1, 2 * WIN - 1), jnp.float32)
    return offset_table


def draw_block_bias(key, part):
    return relative_table(jax.random.fold_in(key, 1))


def draw_grid_bias(key, part):
    return relative_table(jax.random.fold_in(key, 2))


def normal_values(key, dims, scale, limit, held_as=jnp.bfloat16):
    values = jax.random.normal(key, dims, jnp.float32) * scale
    return jnp.minimum(jnp.maximum(values, -limit), limit).astype(held_as)


def setup_inputs(seed: int = 0) -> dict:
    key_list = jax.random.split(jax.random.key(seed), 17)
    pixels = draw_pixels(jax.random.fold_in(key_list[16], 71), 0)
    conv_gain = jnp.clip(1.0 + 0.15 * jax.random.normal(key_list[1], (C,), jnp.float32), 0.25, 1.75)
    expand_weight = normal_values(key_list[2], (C, HID), C ** -0.5, 0.375)
    depth_kernel = normal_values(key_list[3], (3, 3, HID), 9 ** -0.5, 2.0)
    shrink_weight = normal_values(key_list[4], (HID, C), HID ** -0.5, 0.1875)
    block_gain = jnp.clip(1.0 + 0.15 * jax.random.normal(key_list[5], (C,), jnp.float32), 0.25, 1.75)
    block_qkv = normal_values(key_list[6], (C, 3 * C), C ** -0.5, 0.375)
    block_merge = normal_values(key_list[7], (C, C), C ** -0.5, 0.375)
    block_bias = draw_block_bias(jax.random.fold_in(key_list[16], 71), 0)
    grid_gain = jnp.clip(1.0 + 0.15 * jax.random.normal(key_list[9], (C,), jnp.float32), 0.25, 1.75)
    grid_qkv = normal_values(key_list[10], (C, 3 * C), C ** -0.5, 0.375)
    grid_merge = normal_values(key_list[11], (C, C), C ** -0.5, 0.375)
    grid_bias = draw_grid_bias(jax.random.fold_in(key_list[16], 71), 0)
    mlp_gain = jnp.clip(1.0 + 0.15 * jax.random.normal(key_list[13], (C,), jnp.float32), 0.25, 1.75)
    mlp_up = normal_values(key_list[14], (C, HID), C ** -0.5, 0.375)
    mlp_down = normal_values(key_list[15], (HID, C), HID ** -0.5, 0.1875)
    return {"pixels": pixels, "conv_gain": conv_gain, "expand_weight": expand_weight, "depth_kernel": depth_kernel, "shrink_weight": shrink_weight, "block_gain": block_gain, "block_qkv": block_qkv, "block_merge": block_merge, "block_bias": block_bias, "grid_gain": grid_gain, "grid_qkv": grid_qkv, "grid_merge": grid_merge, "grid_bias": grid_bias, "mlp_gain": mlp_gain, "mlp_up": mlp_up, "mlp_down": mlp_down}


epsilon = 1e-05

def layer_norm(values, norm_gain):
    values = values.astype(jnp.float32)
    middle = lax.optimization_barrier(jnp.mean(values, axis=-1, keepdims=True))
    spread = lax.optimization_barrier(jnp.mean(jnp.square(values - middle), axis=-1, keepdims=True))
    return (values - middle) * lax.rsqrt(spread + epsilon) * norm_gain

def project(values, weight):
    return jnp.dot(values, weight, preferred_element_type=jnp.float32)

def widening(normed, weight):
    return jax.nn.gelu(project(normed, weight), approximate=False).astype(jnp.bfloat16)

def relative_bias(offset_table):
    places = jnp.arange(WIN * WIN, dtype=jnp.int32)
    rows_of = places // WIN
    cols_of = places % WIN
    row_index = rows_of[None, :] - rows_of[:, None] + WIN - 1
    col_index = cols_of[None, :] - cols_of[:, None] + WIN - 1
    return offset_table[:, row_index, col_index]

def attend_groups(tokens, norm_gain, qkv_weight, merge_weight, offsets):
    groups = tokens.shape[0]
    flattened = tokens.reshape(groups * WIN * WIN, C)
    normed = layer_norm(flattened, norm_gain).astype(jnp.bfloat16)
    mixture = project(normed, qkv_weight).astype(jnp.bfloat16)
    qkv_parts = mixture.reshape(groups, WIN * WIN, 3, HEADS, HEAD_DIM).astype(jnp.float32)
    scores = jnp.einsum('gqhd,gkhd->ghqk', qkv_parts[:, :, 0], qkv_parts[:, :, 1]) * (1.0 / math.sqrt(HEAD_DIM)) + offsets[None]
    largest = lax.optimization_barrier(jnp.max(scores, axis=-1, keepdims=True))
    raised = jnp.exp(scores - largest)
    weights = (raised / lax.optimization_barrier(jnp.sum(raised, axis=-1, keepdims=True))).astype(jnp.bfloat16)
    head_out = jnp.einsum('ghqk,gkhd->gqhd', weights.astype(jnp.float32), qkv_parts[:, :, 2]).astype(jnp.bfloat16)
    merged = flattened.astype(jnp.float32) + project(head_out.reshape(groups * WIN * WIN, C), merge_weight)
    return merged.astype(jnp.bfloat16).reshape(tokens.shape)

def reference(pixels, conv_gain, expand_weight, depth_kernel, shrink_weight, block_gain, block_qkv, block_merge, block_bias, grid_gain, grid_qkv, grid_merge, grid_bias, mlp_gain, mlp_up, mlp_down):
    picture = jnp.transpose(pixels, (1, 2, 0))
    padded = jnp.pad(picture, ((1, 1), (0, 0), (0, 0)))
    kernel = depth_kernel.astype(jnp.float32)

    def conv_rows(row_start):
        window = lax.dynamic_slice_in_dim(padded, row_start, BAND + 2, 0)
        normed = layer_norm(window, conv_gain).astype(jnp.bfloat16)
        widened = widening(normed.reshape((BAND + 2) * W, C), expand_weight).reshape(BAND + 2, W, HID)
        row_ids = row_start - 1 + jnp.arange(BAND + 2, dtype=jnp.int32)
        inside = (row_ids >= 0) & (row_ids < H)
        widened = jnp.where(inside[:, None, None], widened, jnp.zeros_like(widened))
        widened = jnp.pad(widened, ((0, 0), (1, 1), (0, 0))).astype(jnp.float32)
        summed = jnp.zeros((BAND, W, HID), jnp.float32)
        for row_tap in range(3):
            for col_tap in range(3):
                summed = summed + widened[row_tap:row_tap + BAND, col_tap:col_tap + W] * kernel[row_tap, col_tap]
        depthwise = jax.nn.gelu(summed, approximate=False).astype(jnp.bfloat16)
        centre = lax.dynamic_slice_in_dim(picture, row_start, BAND, 0)
        result = centre.astype(jnp.float32) + project(depthwise.reshape(BAND * W, HID), shrink_weight).reshape(BAND, W, C)
        return result.astype(jnp.bfloat16)
    starts = jnp.arange(H // BAND, dtype=jnp.int32) * BAND
    conv_out = lax.map(conv_rows, starts).reshape(H, W, C)
    block_table = relative_bias(block_bias)

    def block_rows(row_start):
        row_block = lax.dynamic_slice_in_dim(conv_out, row_start, WIN, 0)
        tokens = jnp.transpose(row_block.reshape(WIN, W // WIN, WIN, C), (1, 0, 2, 3)).reshape(W // WIN, WIN * WIN, C)
        attended = attend_groups(tokens, block_gain, block_qkv, block_merge, block_table)
        return jnp.transpose(attended.reshape(W // WIN, WIN, WIN, C), (1, 0, 2, 3)).reshape(WIN, W, C)
    window_starts = jnp.arange(H // WIN, dtype=jnp.int32) * WIN
    block_out = lax.map(block_rows, window_starts).reshape(H, W, C)
    stride_rows = H // WIN
    stride_cols = W // WIN
    arranged = jnp.transpose(block_out.reshape(WIN, stride_rows, WIN, stride_cols, C), (1, 3, 0, 2, 4))
    grid_table = relative_bias(grid_bias)

    def grid_rows(portion):
        tokens = portion.reshape(stride_cols, WIN * WIN, C)
        attended = attend_groups(tokens, grid_gain, grid_qkv, grid_merge, grid_table)
        flattened = attended.reshape(stride_cols * WIN * WIN, C)
        normed = layer_norm(flattened, mlp_gain).astype(jnp.bfloat16)
        hidden = widening(normed, mlp_up)
        finished = (flattened.astype(jnp.float32) + project(hidden, mlp_down)).astype(jnp.bfloat16)
        return finished.reshape(stride_cols, WIN, WIN, C)
    finished = lax.map(grid_rows, arranged)
    picture_out = jnp.transpose(finished, (2, 0, 3, 1, 4)).reshape(H, W, C)
    return jnp.transpose(picture_out, (2, 0, 1))
```

```python
import functools
import math

import jax
import jax.numpy as jnp
import numpy as np
from jax import lax
from jax.experimental import pallas as pl
from jax.experimental.pallas import tpu as pltpu
from jax.sharding import PartitionSpec as P

WIN = 8
HALF = 64
EPS = 1e-05
F32 = jnp.float32
BF16 = jnp.bfloat16
MESH = pl.DeviceIdType.MESH
VM = pl.BlockSpec(memory_space=pltpu.VMEM)
LIMIT = 56 * 1024 * 1024


def dot(a, b, dims=((1,), (0,))):
    return lax.dot_general(a, b, (dims, ((), ())), preferred_element_type=F32)


def norm(values, gain):
    middle = jnp.mean(values, axis=-1, keepdims=True)
    off = values - middle
    spread = jnp.mean(off * off, axis=-1, keepdims=True)
    return (off * lax.rsqrt(spread + EPS) * gain).astype(BF16)


def gelu(v):
    return 0.5 * v * (1.0 + lax.erf(v * np.float32(math.sqrt(0.5))))


def rounded(v):
    return v.astype(BF16).astype(F32)


def swapped(v):
    return pltpu.roll(v, HALF, 1)


def pick_rows(lanes):
    width = 4 * lanes * WIN
    first = np.zeros((lanes * 40, width), np.float32)
    second = np.zeros((lanes * 40, width), np.float32)
    mask = np.zeros((lanes * 40, 128), np.float32)
    for j in range(lanes):
        for q in range(40):
            if q < 32:
                col = (q // 8 * lanes + j) * 8 + q % 8
            else:
                col = ((q - 32) % 4 * lanes + j) * 8 + (-1 if q < 36 else 8)
            row = j * 40 + q
            if col < 0:
                second[row, width - 1] = 1
                mask[row, HALF:] = 1
            elif col >= width:
                second[row, 0] = 1
                mask[row, :HALF] = 1
            else:
                first[row, col] = 1
    return first, second, mask


def prep_body(px, first, second, mask, send):
    half = px.shape[2] // 2
    lanes = send.shape[0]
    for y in range(WIN):
        low, high = px[y, :, :half], px[y, :, half:]
        main = dot(first[...], jnp.concatenate([low, high], 0), ((1,), (1,)))
        rim = dot(second[...], jnp.concatenate([high, low], 0), ((1,), (1,)))
        rows = (main + rim * mask[...]).astype(BF16)
        for j in range(lanes):
            send[j, y] = rows[j * 40 : (j + 1) * 40]


def bias_fill(table, bias):
    t = table[...]
    shifted = [t if z == 0 else pltpu.roll(t, 256 - z * 16, 1) for z in range(WIN)]
    rows = jnp.concatenate([s[:, :128] for s in shifted], 0)
    r = lax.broadcasted_iota(jnp.int32, (128, 128), 0)
    c = lax.broadcasted_iota(jnp.int32, (128, 128), 1)
    m, j = r >> 4, r & 15
    y, x = (c >> 3) & 7, c & 7
    for v in range(WIN):
        onehot = jnp.where((m == 7 - y) & (j == v - x + 7), 1.0, 0.0).astype(F32)
        got = lax.dot_general(
            rows, onehot, (((1,), (0,)), ((), ())),
            precision=lax.Precision.HIGHEST, preferred_element_type=F32,
        )
        bias[:, v] = got.reshape(WIN, WIN, 128)


def attend_pair(x, gain, qkv, merge, bias):
    channels = x.shape[1]
    depth = channels // WIN
    proj = dot(norm(x, gain), qkv)
    q = proj[:, :channels].astype(BF16)
    head = lax.broadcasted_iota(jnp.int32, (WIN, channels), 0)
    place = lax.broadcasted_iota(jnp.int32, (WIN, channels), 1)
    own = jnp.where((place >= head * depth) & (place < head * depth + depth), 1.0, 0.0)

    def spread(rows):
        wide = rounded(rows)[:, None, :] * own[None]
        return wide.reshape(64 * WIN, channels).astype(BF16)

    keys = [spread(proj[w * 64 : w * 64 + 64, channels : 2 * channels]) for w in (0, 1)]
    vals = [spread(proj[w * 64 : w * 64 + 64, 2 * channels :]) for w in (0, 1)]
    raw = [dot(k, q, ((1,), (1,))) for k in keys]
    lane = lax.broadcasted_iota(jnp.int32, raw[0].shape, 1)
    scores = jnp.where(lane < 64, raw[0], raw[1]) * np.float32(1.0 / math.sqrt(depth))
    scores = scores.reshape(64, WIN, 128) + bias[...].reshape(64, WIN, 128)
    raised = jnp.exp(scores - jnp.max(scores, axis=0, keepdims=True))
    weights = raised * (1.0 / jnp.sum(raised, axis=0, keepdims=True))
    weights = jnp.transpose(weights.reshape(512, 128)).astype(BF16)
    heads = jnp.concatenate([dot(weights[w * 64 : w * 64 + 64], vals[w]) for w in (0, 1)], 0)
    return rounded(x + dot(heads.astype(BF16), merge))


def block_body(
    edge, got, conv_gain, expand, taps, shrink, gain, qkv, merge, table, send,
    tokens, normed, acc, bias, done,
):
    lanes = got.shape[0]
    lane = lax.broadcasted_iota(jnp.int32, (400, 128), 1)
    row = lax.broadcasted_iota(jnp.int32, (400, 128), 0)
    keep = ((row >= 40) | (edge[0] == 0)) & ((row < 360) | (edge[1] == 0))
    for i in range(0, lanes, 2):
        a = jnp.where(keep, got[i].astype(F32).reshape(400, 128), 0.0)
        b = jnp.where(keep, got[i + 1].astype(F32).reshape(400, 128), 0.0)
        cols = slice(i * HALF, i * HALF + 128)
        tokens[:400, cols] = jnp.where(lane < HALF, a, swapped(b))
        tokens[400:, cols] = jnp.where(lane < HALF, swapped(a), b)
    for half in (0, 1):
        normed[half * 400 : half * 400 + 400] = norm(
            tokens[half * 400 : half * 400 + 400], conv_gain[...]
        )
    for half in (0, 1):
        for y in range(WIN):
            base = half * 400 + (y + 1) * 40
            acc[half * 256 + y * 32 : half * 256 + y * 32 + 32] = tokens[base : base + 32]

    width = 128
    inner = lax.broadcasted_iota(jnp.int32, (WIN, WIN, width), 1)

    def chunk(n, _):
        at = pl.ds(pl.multiple_of(n * width, width), width)
        kernel = taps[:, at]
        for half in (0, 1):
            wide = rounded(gelu(dot(normed[half * 400 : half * 400 + 400], expand[:, at])))
            wide = wide.reshape(10, 5, 8, width)

            def column(v, tile):
                total = None
                for u in range(3):
                    term = wide[u : u + WIN, tile] * kernel[u * 3 + v][None, None, :]
                    total = term if total is None else total + term
                return total

            left_rim, right_rim = column(0, 4), column(2, 4)
            parts = []
            for b in range(4):
                left = jnp.where(
                    inner == 0, left_rim[:, b : b + 1], pltpu.roll(column(0, b), 1, 1)
                )
                right = jnp.where(
                    inner == 7, right_rim[:, 4 + b : 5 + b], pltpu.roll(column(2, b), 7, 1)
                )
                parts.append(column(1, b) + left + right)
            summed = jnp.stack(parts, axis=1).reshape(256, width)
            narrow = dot(gelu(summed).astype(BF16), shrink[at, :])
            acc[half * 256 : half * 256 + 256] += narrow
        return _

    lax.fori_loop(0, expand.shape[1] // width, chunk, 0)
    bias_fill(table, bias)
    channels = acc.shape[1]

    def pair(n, _):
        groups = []
        for w in (0, 1):
            b = n * 2 + w
            base = (b >> 2) * 256 + (b & 3) * 8
            groups += [acc[pl.ds(pl.multiple_of(base + y * 32, 8), 8)] for y in range(WIN)]
        x = rounded(jnp.concatenate(groups, 0))
        out = attend_pair(x, gain[...], qkv[...], merge[...], bias)
        for w in (0, 1):
            b = n * 2 + w
            for y in range(WIN):
                here = slice(w * 64 + y * 8, w * 64 + y * 8 + 8)
                at = pl.ds(pl.multiple_of(y * 64 + b * 8, 8), 8)
                for c in range(channels // 128):
                    done[c, at] = out[here, c * 128 : c * 128 + 128]
        return _

    lax.fori_loop(0, 4, pair, 0)
    for x in range(WIN):
        for c in range(channels // 128):
            part = done[c, pl.ds(x, 64, stride=8)]
            send[x, :, c * 128 : c * 128 + 128] = part.astype(BF16)


def grid_body(got, gain, qkv, merge, table, mlp_gain, up, down, send, tokens, bias):
    for a in range(WIN):
        tokens[a] = got[a].astype(F32)
    bias_fill(table, bias)
    channels = tokens.shape[2]
    lane = lax.broadcasted_iota(jnp.int32, (64, 128), 1)

    def pair(n, _):
        halves = [
            tokens[:, pl.ds(pl.multiple_of(n * 8 + w * 32, 8), 8)].reshape(64, channels)
            for w in (0, 1)
        ]
        x = attend_pair(
            jnp.concatenate(halves, 0), gain[...], qkv[...], merge[...], bias
        )
        hidden = gelu(dot(norm(x, mlp_gain[...]), up[...])).astype(BF16)
        out = rounded(x + dot(hidden, down[...]))
        for c in range(0, channels, 128):
            low, high = out[:64, c : c + 128], out[64:, c : c + 128]
            even = jnp.where(lane < HALF, low, swapped(high))
            odd = jnp.where(lane < HALF, swapped(low), high)
            j = c // HALF
            send[:, j, n] = even.reshape(WIN, WIN, 128).astype(BF16)
            send[:, j + 1, n] = odd.reshape(WIN, WIN, 128).astype(BF16)
        return _

    lax.fori_loop(0, 4, pair, 0)


def finish_body(got, out, rows):
    lanes = got.shape[1]
    columns = WIN * WIN * lanes
    for x in range(WIN):
        for j in range(lanes):
            rows[pl.ds(j * 8 + x, 32, stride=8 * lanes)] = got[x, j].astype(F32).reshape(32, 128)
    for y in range(4):
        flat = jnp.transpose(rows[y * columns : (y + 1) * columns]).astype(BF16)
        out[y] = flat[:HALF]
        out[y + 4] = flat[HALF:]


def greet(partners):
    barrier = pltpu.get_barrier_semaphore()
    for partner in partners:
        pl.semaphore_signal(barrier, inc=1, device_id=partner, device_id_type=MESH)
    pl.semaphore_wait(barrier, len(partners))


def spread_body(bands, lanes, send, got, send_sem, recv_sem, own_sem):
    band, lane = lax.axis_index("rows"), lax.axis_index("ch")
    below, above = lax.rem(band + 1, bands), lax.rem(band + bands - 1, bands)
    others = [lax.rem(lane + d, lanes) for d in range(1, lanes)]
    everyone = [lax.rem(lane + d, lanes) for d in range(lanes)]
    greet(
        [(band, j) for j in others]
        + [(below, j) for j in everyone]
        + [(above, j) for j in everyone]
    )

    def remote(j, d, kind, row, source, mine):
        if kind == 0:
            src, dst = send.at[j], got.at[mine, pl.ds(1, WIN)]
        else:
            src = send.at[j, WIN - 1 if kind == 1 else 0]
            dst = got.at[mine, 0 if kind == 1 else WIN + 1]
        return pltpu.make_async_remote_copy(
            src_ref=src, dst_ref=dst, send_sem=send_sem.at[kind, d],
            recv_sem=recv_sem.at[kind, mine], device_id=(row, j), device_id_type=MESH,
        )

    copies = []
    for d in range(1, lanes):
        copies.append(remote(lax.rem(lane + d, lanes), d, 0, band, None, lane))
    for kind, row in ((1, below), (2, above)):
        for d in range(lanes):
            copies.append(remote(lax.rem(lane + d, lanes), d, kind, row, None, lane))
    for copy in copies:
        copy.start()
    own = pltpu.make_async_copy(send.at[lane], got.at[lane, pl.ds(1, WIN)], own_sem)
    own.start()
    own.wait()
    for d in range(1, lanes):
        j = lax.rem(lane + d, lanes)
        remote(j, d, 0, band, None, j).wait_recv()
    for kind, row in ((1, below), (2, above)):
        for d in range(lanes):
            j = lax.rem(lane + d, lanes)
            remote(j, d, kind, row, None, j).wait_recv()
    for copy in copies:
        copy.wait_send()


def regroup_body(step, send, got, send_sem, recv_sem, own_sem):
    band, lane = lax.axis_index("rows"), lax.axis_index("ch")
    slot, rest = band // step, lax.rem(band, step)
    slots = [lax.rem(slot + d, WIN) for d in range(WIN)]
    greet([(s * step + rest, lane) for s in slots[1:]])

    def remote(d, mine):
        return pltpu.make_async_remote_copy(
            src_ref=send.at[slots[d]], dst_ref=got.at[mine], send_sem=send_sem.at[d],
            recv_sem=recv_sem.at[mine], device_id=(slots[d] * step + rest, lane),
            device_id_type=MESH,
        )

    copies = [remote(d, slot) for d in range(1, WIN)]
    for copy in copies:
        copy.start()
    own = pltpu.make_async_copy(send.at[slot], got.at[slot], own_sem)
    own.start()
    own.wait()
    for d in range(1, WIN):
        remote(d, slots[d]).wait_recv()
    for copy in copies:
        copy.wait_send()


def home_body(step, lanes, send, got, send_sem, recv_sem, own_sem):
    band, lane = lax.axis_index("rows"), lax.axis_index("ch")
    slot, rest = band // step, lax.rem(band, step)
    peers = [
        (d, e, lax.rem(slot + d, WIN), lax.rem(lane + e, lanes))
        for d in range(WIN)
        for e in range(lanes)
        if d or e
    ]
    greet([(s * step + rest, j) for _, _, s, j in peers])

    def remote(d, e, s, j, slot_at, lane_at):
        return pltpu.make_async_remote_copy(
            src_ref=send.at[s, j], dst_ref=got.at[slot_at, lane_at],
            send_sem=send_sem.at[d, e], recv_sem=recv_sem.at[slot_at, lane_at],
            device_id=(s * step + rest, j), device_id_type=MESH,
        )

    copies = [remote(d, e, s, j, slot, lane) for d, e, s, j in peers]
    for copy in copies:
        copy.start()
    own = pltpu.make_async_copy(send.at[slot, lane], got.at[slot, lane], own_sem)
    own.start()
    own.wait()
    for d, e, s, j in peers:
        remote(d, e, s, j, s, j).wait_recv()
    for copy in copies:
        copy.wait_send()


def local(body, name, shape, dtype, operands, scratch, smem=0):
    return pl.pallas_call(
        body,
        out_shape=jax.ShapeDtypeStruct(shape, dtype),
        in_specs=[pl.BlockSpec(memory_space=pltpu.SMEM)] * smem + [VM] * (len(operands) - smem),
        out_specs=VM,
        scratch_shapes=scratch,
        compiler_params=pltpu.CompilerParams(vmem_limit_bytes=LIMIT),
        name=name,
    )(*operands)


def exchange(body, name, number, shape, operand, sems):
    return pl.pallas_call(
        body,
        out_shape=jax.ShapeDtypeStruct(shape, BF16),
        in_specs=[VM],
        out_specs=VM,
        scratch_shapes=[
            pltpu.SemaphoreType.DMA(sems),
            pltpu.SemaphoreType.DMA(sems),
            pltpu.SemaphoreType.DMA,
        ],
        compiler_params=pltpu.CompilerParams(
            collective_id=number, has_side_effects=True, vmem_limit_bytes=LIMIT
        ),
        name=name,
    )(operand)


def flat_table(bias):
    return jnp.pad(bias, ((0, 0), (0, 1), (0, 1))).reshape(bias.shape[0], 256)


def shards(
    pixels, conv_gain, expand_weight, depth_kernel, shrink_weight,
    block_gain, block_qkv, block_merge, block_bias,
    grid_gain, grid_qkv, grid_merge, grid_bias, mlp_gain, mlp_up, mlp_down,
):
    lanes, bands = lax.axis_size("ch"), lax.axis_size("rows")
    channels = expand_weight.shape[0]
    hidden = expand_weight.shape[1]
    columns = pixels.shape[2]
    step = bands // WIN
    band = lax.axis_index("rows")
    edge = jnp.stack([band == 0, band == bands - 1]).astype(jnp.int32)
    first, second, mask = pick_rows(lanes)
    px = jnp.transpose(pixels, (1, 0, 2))
    sent = local(
        prep_body, "prep", (lanes, WIN, 40, 128), BF16,
        [px, jnp.asarray(first, BF16), jnp.asarray(second, BF16), jnp.asarray(mask, F32)], [],
    )
    got = exchange(
        functools.partial(spread_body, bands, lanes), "spread", 1,
        (lanes, WIN + 2, 40, 128), sent, (3, lanes),
    )
    taps = depth_kernel.astype(F32).reshape(9, hidden)
    sent = local(
        block_body, "block", (WIN, 64, channels), BF16,
        [
            edge, got, conv_gain[None], expand_weight, taps, shrink_weight,
            block_gain[None], block_qkv, block_merge, flat_table(block_bias),
        ],
        [
            pltpu.VMEM((800, channels), F32),
            pltpu.VMEM((800, channels), BF16),
            pltpu.VMEM((512, channels), F32),
            pltpu.VMEM((WIN, WIN, WIN, 128), F32),
            pltpu.VMEM((channels // 128, 512, 128), F32),
        ],
        smem=1,
    )
    got = exchange(
        functools.partial(regroup_body, step), "regroup", 2, sent.shape, sent, (WIN,)
    )
    sent = local(
        grid_body, "grid", (WIN, lanes, 4, WIN, 128), BF16,
        [
            got, grid_gain[None], grid_qkv, grid_merge, flat_table(grid_bias),
            mlp_gain[None], mlp_up, mlp_down,
        ],
        [
            pltpu.VMEM((WIN, 64, channels), F32),
            pltpu.VMEM((WIN, WIN, WIN, 128), F32),
        ],
    )
    got = exchange(
        functools.partial(home_body, step, lanes), "home", 3, sent.shape, sent, (WIN, lanes)
    )
    out = local(
        finish_body, "finish", (WIN, HALF, columns), BF16, [got],
        [pltpu.VMEM((4 * columns, 128), F32)],
    )
    return jnp.transpose(out, (1, 0, 2))


def solution(mesh):
    in_specs = (P("ch", "rows", None),) + (P(),) * 15
    return jax.shard_map(
        shards, mesh=mesh, in_specs=in_specs, out_specs=P("ch", "rows", None), check_vma=False
    )
```

```python
import functools
import math

import jax
import jax.numpy as jnp
import numpy as np
from jax import lax
from jax.experimental import pallas as pl
from jax.experimental.pallas import tpu as pltpu
from jax.sharding import PartitionSpec as P

WIN = 8
HALF = 64
EPS = 1e-05
F32 = jnp.float32
BF16 = jnp.bfloat16
MESH = pl.DeviceIdType.MESH
VM = pl.BlockSpec(memory_space=pltpu.VMEM)
LIMIT = 56 * 1024 * 1024


def dot(a, b, dims=((1,), (0,))):
    return lax.dot_general(a, b, (dims, ((), ())), preferred_element_type=F32)


def norm(values, gain):
    middle = jnp.mean(values, axis=-1, keepdims=True)
    off = values - middle
    spread = jnp.mean(off * off, axis=-1, keepdims=True)
    return (off * lax.rsqrt(spread + EPS) * gain).astype(BF16)


def gelu(v):
    return 0.5 * v * (1.0 + lax.erf(v * np.float32(math.sqrt(0.5))))


def rounded(v):
    return v.astype(BF16).astype(F32)


def swapped(v):
    return pltpu.roll(v, HALF, 1)


def pick_rows(lanes):
    width = 4 * lanes * WIN
    first = np.zeros((lanes * 40, width), np.float32)
    second = np.zeros((lanes * 40, width), np.float32)
    mask = np.zeros((lanes * 40, 128), np.float32)
    for j in range(lanes):
        for q in range(40):
            if q < 32:
                col = (q // 8 * lanes + j) * 8 + q % 8
            else:
                col = ((q - 32) % 4 * lanes + j) * 8 + (-1 if q < 36 else 8)
            row = j * 40 + q
            if col < 0:
                second[row, width - 1] = 1
                mask[row, HALF:] = 1
            elif col >= width:
                second[row, 0] = 1
                mask[row, :HALF] = 1
            else:
                first[row, col] = 1
    return first, second, mask


def prep_body(px, first, second, mask, send):
    half = px.shape[2] // 2
    lanes = send.shape[0]
    for y in range(WIN):
        low, high = px[y, :, :half], px[y, :, half:]
        main = dot(first[...], jnp.concatenate([low, high], 0), ((1,), (1,)))
        rim = dot(second[...], jnp.concatenate([high, low], 0), ((1,), (1,)))
        rows = (main + rim * mask[...]).astype(BF16)
        for j in range(lanes):
            send[j, y] = rows[j * 40 : (j + 1) * 40]


def bias_fill(table, flat, bias):
    flat[...] = jnp.zeros_like(flat)
    for i in range(2 * WIN - 1):
        flat[:, i * 16 : i * 16 + 15] = table[:, i, :]
    t = flat[...]
    shifted = [t if z == 0 else pltpu.roll(t, 256 - z * 16, 1) for z in range(WIN)]
    rows = jnp.concatenate([s[:, :128] for s in shifted], 0)
    r = lax.broadcasted_iota(jnp.int32, (128, 128), 0)
    c = lax.broadcasted_iota(jnp.int32, (128, 128), 1)
    m, j = r >> 4, r & 15
    y, x = (c >> 3) & 7, c & 7
    for v in range(WIN):
        onehot = jnp.where((m == 7 - y) & (j == v - x + 7), 1.0, 0.0).astype(F32)
        got = lax.dot_general(
            rows, onehot, (((1,), (0,)), ((), ())),
            precision=lax.Precision.HIGHEST, preferred_element_type=F32,
        )
        bias[:, v] = got.reshape(WIN, WIN, 128)


def attend_pair(x, gain, qkv, merge, bias):
    channels = x.shape[1]
    depth = channels // WIN
    proj = dot(norm(x, gain), qkv)
    q = proj[:, :channels].astype(BF16)
    head = lax.broadcasted_iota(jnp.int32, (WIN, channels), 0)
    place = lax.broadcasted_iota(jnp.int32, (WIN, channels), 1)
    own = jnp.where((place >= head * depth) & (place < head * depth + depth), 1.0, 0.0)

    def spread(rows):
        wide = rounded(rows)[:, None, :] * own[None]
        return wide.reshape(64 * WIN, channels).astype(BF16)

    keys = [spread(proj[w * 64 : w * 64 + 64, channels : 2 * channels]) for w in (0, 1)]
    vals = [spread(proj[w * 64 : w * 64 + 64, 2 * channels :]) for w in (0, 1)]
    raw = [dot(k, q, ((1,), (1,))) for k in keys]
    lane = lax.broadcasted_iota(jnp.int32, raw[0].shape, 1)
    scores = jnp.where(lane < 64, raw[0], raw[1]) * np.float32(1.0 / math.sqrt(depth))
    scores = scores.reshape(64, WIN, 128) + bias[...].reshape(64, WIN, 128)
    raised = jnp.exp(scores - jnp.max(scores, axis=0, keepdims=True))
    weights = raised * (1.0 / jnp.sum(raised, axis=0, keepdims=True))
    weights = jnp.transpose(weights.reshape(512, 128)).astype(BF16)
    heads = jnp.concatenate([dot(weights[w * 64 : w * 64 + 64], vals[w]) for w in (0, 1)], 0)
    return rounded(x + dot(heads.astype(BF16), merge))


def conv_phase(at_top, at_end, got, gain, expand, taps, shrink, tokens, normed, acc):
    lanes = got.shape[0]
    lane = lax.broadcasted_iota(jnp.int32, (400, 128), 1)
    row = lax.broadcasted_iota(jnp.int32, (400, 128), 0)
    lowest = jnp.where(at_top, 40, 0)
    highest = jnp.where(at_end, 360, 400)
    keep = (row >= lowest) & (row < highest)
    for i in range(0, lanes, 2):
        a = jnp.where(keep, got[i].astype(F32).reshape(400, 128), 0.0)
        b = jnp.where(keep, got[i + 1].astype(F32).reshape(400, 128), 0.0)
        cols = slice(i * HALF, i * HALF + 128)
        tokens[:400, cols] = jnp.where(lane < HALF, a, swapped(b))
        tokens[400:, cols] = jnp.where(lane < HALF, swapped(a), b)
    for half in (0, 1):
        normed[half * 400 : half * 400 + 400] = norm(
            tokens[half * 400 : half * 400 + 400], gain[...]
        )
    for half in (0, 1):
        for y in range(WIN):
            base = half * 400 + (y + 1) * 40
            acc[half * 256 + y * 32 : half * 256 + y * 32 + 32] = tokens[base : base + 32]

    width = 128
    inner = lax.broadcasted_iota(jnp.int32, (WIN, WIN, width), 1)

    def chunk(n, _):
        at = pl.ds(pl.multiple_of(n * width, width), width)
        kernel = taps[:, :, at].astype(F32)
        for half in (0, 1):
            wide = rounded(gelu(dot(normed[half * 400 : half * 400 + 400], expand[:, at])))
            wide = wide.reshape(10, 5, 8, width)

            def column(v, tile):
                total = None
                for u in range(3):
                    term = wide[u : u + WIN, tile] * kernel[u, v][None, None, :]
                    total = term if total is None else total + term
                return total

            left_rim, right_rim = column(0, 4), column(2, 4)
            parts = []
            for b in range(4):
                left = jnp.where(
                    inner == 0, left_rim[:, b : b + 1], pltpu.roll(column(0, b), 1, 1)
                )
                right = jnp.where(
                    inner == 7, right_rim[:, 4 + b : 5 + b], pltpu.roll(column(2, b), 7, 1)
                )
                parts.append(column(1, b) + left + right)
            summed = jnp.stack(parts, axis=1).reshape(256, width)
            narrow = dot(gelu(summed).astype(BF16), shrink[at, :])
            acc[half * 256 : half * 256 + 256] += narrow
        return _

    lax.fori_loop(0, expand.shape[1] // width, chunk, 0)


def window_pair(n, gain, qkv, merge, bias, acc, done, send):
    channels = acc.shape[1]
    groups = []
    for w in (0, 1):
        b = n * 2 + w
        base = (b >> 2) * 256 + (b & 3) * 8
        groups += [acc[pl.ds(pl.multiple_of(base + y * 32, 8), 8)] for y in range(WIN)]
    x = rounded(jnp.concatenate(groups, 0))
    out = attend_pair(x, gain[...], qkv[...], merge[...], bias)
    for c in range(channels // 128):
        cols = slice(c * 128, c * 128 + 128)
        done[c] = out[:, cols]
        for x in range(WIN):
            send[x, n, :, cols] = done[c, pl.ds(x, 16, stride=8)].astype(BF16)


def group_pair(n, gain, qkv, merge, bias, mlp_gain, up, down, tokens, send):
    parts = tokens.shape[0]
    lane = lax.broadcasted_iota(jnp.int32, (64, 128), 1)
    halves = [
        jnp.concatenate([tokens[c, pl.ds(n + w * 4, 64, stride=8)] for c in range(parts)], 1)
        for w in (0, 1)
    ]
    x = attend_pair(jnp.concatenate(halves, 0), gain[...], qkv[...], merge[...], bias)
    hidden = gelu(dot(norm(x, mlp_gain[...]), up[...])).astype(BF16)
    out = rounded(x + dot(hidden, down[...]))
    for c in range(parts):
        low, high = out[:64, c * 128 : c * 128 + 128], out[64:, c * 128 : c * 128 + 128]
        even = jnp.where(lane < HALF, low, swapped(high))
        odd = jnp.where(lane < HALF, swapped(low), high)
        send[:, 2 * c, n] = even.reshape(WIN, WIN, 128).astype(BF16)
        send[:, 2 * c + 1, n] = odd.reshape(WIN, WIN, 128).astype(BF16)


def finish_chunk(n, got, rows, out):
    lanes = got.shape[1]
    for x in range(WIN):
        for j in range(lanes):
            rows[pl.ds(j * 8 + x, 8, stride=8 * lanes)] = got[x, j, n].astype(F32)
    flat = jnp.transpose(rows[...]).astype(BF16)
    out[n] = flat[:HALF]
    out[n + 4] = flat[HALF:]


def whole_body(
    bands, lanes,
    px, first, second, mask, conv_gain, expand, taps, shrink,
    block_gain, block_qkv, block_merge, block_table,
    grid_gain, grid_qkv, grid_merge, grid_table, mlp_gain, up, down,
    out,
    send0, got0, tokens, normed, acc, flat, block_bias, grid_bias, done,
    send1, got1, columns, send2, got2, rows,
    ss0, rs0, os0, ss1, rs1, os1, ss2, rs2, os2,
):
    band, lane = lax.axis_index("rows"), lax.axis_index("ch")
    step = bands // WIN
    slot, rest = band // step, lax.rem(band, step)
    below, above = lax.rem(band + 1, bands), lax.rem(band + bands - 1, bands)
    lane_at = [lax.rem(lane + d, lanes) for d in range(lanes)]
    slot_at = [lax.rem(slot + d, WIN) for d in range(WIN)]
    band_at = [s * step + rest for s in slot_at]
    pairs = [(d, e) for d in range(WIN) for e in range(lanes) if d or e]
    barrier = pltpu.get_barrier_semaphore()
    partners = [(row, j) for row in (below, above) for j in lane_at]
    partners += [(band_at[d], lane_at[e]) for d, e in pairs]
    for partner in partners:
        pl.semaphore_signal(barrier, inc=1, device_id=partner, device_id_type=MESH)
    prep_body(px, first, second, mask, send0)
    pl.semaphore_wait(barrier, len(partners))

    def spread(kind, d, mine):
        row = (band, below, above)[kind]
        if kind == 0:
            src, dst = send0.at[lane_at[d]], got0.at[mine, pl.ds(1, WIN)]
        else:
            src = send0.at[lane_at[d], WIN - 1 if kind == 1 else 0]
            dst = got0.at[mine, 0 if kind == 1 else WIN + 1]
        return pltpu.make_async_remote_copy(
            src_ref=src, dst_ref=dst, send_sem=ss0.at[kind, d], recv_sem=rs0.at[kind, mine],
            device_id=(row, lane_at[d]), device_id_type=MESH,
        )

    spreads = [(k, d) for k in range(3) for d in range(lanes) if k or d]
    for k, d in spreads:
        spread(k, d, lane).start()
    own = pltpu.make_async_copy(send0.at[lane], got0.at[lane, pl.ds(1, WIN)], os0)
    own.start()
    bias_fill(block_table, flat, block_bias)
    bias_fill(grid_table, flat, grid_bias)
    own.wait()
    for k, d in spreads:
        spread(k, d, lane_at[d]).wait_recv()
    conv_phase(
        band == 0, band == bands - 1, got0, conv_gain, expand, taps, shrink, tokens, normed, acc
    )

    def regroup(n, d, mine):
        return pltpu.make_async_remote_copy(
            src_ref=send1.at[slot_at[d], n], dst_ref=got1.at[mine, n],
            send_sem=ss1.at[n, d], recv_sem=rs1.at[n, mine],
            device_id=(band_at[d], lane), device_id_type=MESH,
        )

    def regroup_own(n):
        return pltpu.make_async_copy(send1.at[slot, n], got1.at[slot, n], os1.at[n])

    def windows(n, _):
        window_pair(n, block_gain, block_qkv, block_merge, block_bias, acc, done, send1)
        for d in range(1, WIN):
            regroup(n, d, slot).start()
        regroup_own(n).start()
        return _

    lax.fori_loop(0, 4, windows, 0)

    def arrive(n, _):
        regroup_own(n).wait()
        for d in range(1, WIN):
            regroup(n, d, slot_at[d]).wait_recv()
        for a in range(WIN):
            part = got1[a, n].astype(F32)
            for c in range(columns.shape[0]):
                columns[c, pl.ds(pl.multiple_of(a * 64 + n * 16, 16), 16)] = part[
                    :, c * 128 : c * 128 + 128
                ]
        return _

    lax.fori_loop(0, 4, arrive, 0)

    def home(n, d, e, from_slot, from_lane):
        return pltpu.make_async_remote_copy(
            src_ref=send2.at[slot_at[d], lane_at[e], n], dst_ref=got2.at[from_slot, from_lane, n],
            send_sem=ss2.at[n, d, e], recv_sem=rs2.at[n, from_slot, from_lane],
            device_id=(band_at[d], lane_at[e]), device_id_type=MESH,
        )

    def home_own(n):
        return pltpu.make_async_copy(
            send2.at[slot, lane, n], got2.at[slot, lane, n], os2.at[n]
        )

    def groups(n, _):
        group_pair(
            n, grid_gain, grid_qkv, grid_merge, grid_bias, mlp_gain, up, down, columns, send2
        )
        for d, e in pairs:
            home(n, d, e, slot, lane).start()
        home_own(n).start()
        return _

    lax.fori_loop(0, 4, groups, 0)

    def finish(n, _):
        home_own(n).wait()
        for d, e in pairs:
            home(n, d, e, slot_at[d], lane_at[e]).wait_recv()
        finish_chunk(n, got2, rows, out)
        return _

    lax.fori_loop(0, 4, finish, 0)
    for k, d in spreads:
        spread(k, d, lane).wait_send()

    def sent(n, _):
        for d in range(1, WIN):
            regroup(n, d, slot).wait_send()
        for d, e in pairs:
            home(n, d, e, slot, lane).wait_send()
        return _

    lax.fori_loop(0, 4, sent, 0)


def shards(
    pixels, conv_gain, expand_weight, depth_kernel, shrink_weight,
    block_gain, block_qkv, block_merge, block_bias,
    grid_gain, grid_qkv, grid_merge, grid_bias, mlp_gain, mlp_up, mlp_down,
):
    lanes, bands = lax.axis_size("ch"), lax.axis_size("rows")
    channels = expand_weight.shape[0]
    columns = pixels.shape[2]
    first, second, mask = pick_rows(lanes)
    operands = [
        jnp.transpose(pixels, (1, 0, 2)),
        jnp.asarray(first, BF16), jnp.asarray(second, BF16), jnp.asarray(mask, F32),
        conv_gain[None], expand_weight, depth_kernel, shrink_weight,
        block_gain[None], block_qkv, block_merge, block_bias,
        grid_gain[None], grid_qkv, grid_merge, grid_bias,
        mlp_gain[None], mlp_up, mlp_down,
    ]
    dma = pltpu.SemaphoreType.DMA
    out = pl.pallas_call(
        functools.partial(whole_body, bands, lanes),
        out_shape=jax.ShapeDtypeStruct((WIN, HALF, columns), BF16),
        in_specs=[VM] * len(operands),
        out_specs=VM,
        scratch_shapes=[
            pltpu.VMEM((lanes, WIN, 40, 128), BF16),
            pltpu.VMEM((lanes, WIN + 2, 40, 128), BF16),
            pltpu.VMEM((800, channels), F32),
            pltpu.VMEM((800, channels), BF16),
            pltpu.VMEM((512, channels), F32),
            pltpu.VMEM((WIN, 256), F32),
            pltpu.VMEM((WIN, WIN, WIN, 128), F32),
            pltpu.VMEM((WIN, WIN, WIN, 128), F32),
            pltpu.VMEM((channels // 128, 128, 128), F32),
            pltpu.VMEM((WIN, 4, 16, channels), BF16),
            pltpu.VMEM((WIN, 4, 16, channels), BF16),
            pltpu.VMEM((channels // 128, 512, 128), F32),
            pltpu.VMEM((WIN, lanes, 4, WIN, 128), BF16),
            pltpu.VMEM((WIN, lanes, 4, WIN, 128), BF16),
            pltpu.VMEM((columns, 128), F32),
            dma((3, lanes)), dma((3, lanes)), dma,
            dma((4, WIN)), dma((4, WIN)), dma((4,)),
            dma((4, WIN, lanes)), dma((4, WIN, lanes)), dma((4,)),
        ],
        compiler_params=pltpu.CompilerParams(
            collective_id=1, has_side_effects=True, vmem_limit_bytes=LIMIT
        ),
        name="maxvit",
    )(*operands)
    return jnp.transpose(out, (1, 0, 2))


def solution(mesh):
    in_specs = (P("ch", "rows", None),) + (P(),) * 15
    return jax.shard_map(
        shards, mesh=mesh, in_specs=in_specs, out_specs=P("ch", "rows", None), check_vma=False
    )
```

```python
import functools
import math

import jax
import jax.numpy as jnp
import numpy as np
from jax import lax
from jax.experimental import pallas as pl
from jax.experimental.pallas import tpu as pltpu
from jax.sharding import PartitionSpec as P

WIN = 8
HALF = 64
EPS = 1e-05
F32 = jnp.float32
BF16 = jnp.bfloat16
MESH = pl.DeviceIdType.MESH
VM = pl.BlockSpec(memory_space=pltpu.VMEM)
LIMIT = 56 * 1024 * 1024


def dot(a, b, dims=((1,), (0,))):
    return lax.dot_general(a, b, (dims, ((), ())), preferred_element_type=F32)


def norm(values, gain):
    middle = jnp.mean(values, axis=-1, keepdims=True)
    off = values - middle
    spread = jnp.mean(off * off, axis=-1, keepdims=True)
    return (off * lax.rsqrt(spread + EPS) * gain).astype(BF16)


def twice_gelu(v):
    return v * (1.0 + lax.erf(v * np.float32(math.sqrt(0.5))))


def rounded(v):
    return v.astype(BF16).astype(F32)


def swapped(v):
    return pltpu.roll(v, HALF, 1)


def pick_rows(lanes):
    width = 4 * lanes * WIN
    first = np.zeros((lanes * 40, width), np.float32)
    second = np.zeros((lanes * 40, width), np.float32)
    mask = np.zeros((lanes * 40, 128), np.float32)
    for j in range(lanes):
        for q in range(40):
            if q < 32:
                col = (q // 8 * lanes + j) * 8 + q % 8
            else:
                col = ((q - 32) % 4 * lanes + j) * 8 + (-1 if q < 36 else 8)
            row = j * 40 + q
            if col < 0:
                second[row, width - 1] = 1
                mask[row, HALF:] = 1
            elif col >= width:
                second[row, 0] = 1
                mask[row, :HALF] = 1
            else:
                first[row, col] = 1
    return first, second, mask


def prep_body(px, first, second, mask, plane, send):
    half = px.shape[2] // 2
    lanes = send.shape[0]
    for c in range(plane.shape[0]):
        part = px[:, :, c * 128 : c * 128 + 128].astype(F32)
        plane[c] = part.reshape(HALF * WIN, 128)
    for y in range(WIN):
        line = [plane[c, pl.ds(y, HALF, stride=WIN)] for c in range(plane.shape[0])]
        line = jnp.concatenate(line, 1).astype(BF16)
        low, high = line[:, :half], line[:, half:]
        main = dot(first[...], jnp.concatenate([low, high], 0), ((1,), (1,)))
        rim = dot(second[...], jnp.concatenate([high, low], 0), ((1,), (1,)))
        rows = (main + rim * mask[...]).astype(BF16)
        for j in range(lanes):
            send[j, y] = rows[j * 40 : (j + 1) * 40]


def bias_fill(table, flat, bias):
    flat[...] = jnp.zeros_like(flat)
    for i in range(2 * WIN - 1):
        flat[:, i * 16 : i * 16 + 15] = table[i]
    t = flat[...]
    shifted = [t if z == 0 else pltpu.roll(t, 256 - z * 16, 1) for z in range(WIN)]
    rows = jnp.concatenate([s[:, :128] for s in shifted], 0)
    r = lax.broadcasted_iota(jnp.int32, (128, 128), 0)
    c = lax.broadcasted_iota(jnp.int32, (128, 128), 1)
    m, j = r >> 4, r & 15
    y, x = (c >> 3) & 7, c & 7
    for v in range(WIN):
        onehot = jnp.where((m == 7 - y) & (j == v - x + 7), 1.0, 0.0).astype(F32)
        got = lax.dot_general(
            rows, onehot, (((1,), (0,)), ((), ())),
            precision=lax.Precision.HIGHEST, preferred_element_type=F32,
        )
        bias[:, v] = got.reshape(WIN, WIN, 128)


def attend_pair(x, gain, qkv, merge, bias):
    channels = x.shape[1]
    depth = channels // WIN
    proj = dot(norm(x, gain), qkv)
    q = proj[:, :channels].astype(BF16)
    head = lax.broadcasted_iota(jnp.int32, (WIN, channels), 0)
    place = lax.broadcasted_iota(jnp.int32, (WIN, channels), 1)
    own = jnp.where((place >= head * depth) & (place < head * depth + depth), 1.0, 0.0)

    def spread(rows):
        wide = rounded(rows)[:, None, :] * own[None]
        return wide.reshape(64 * WIN, channels).astype(BF16)

    keys = [spread(proj[w * 64 : w * 64 + 64, channels : 2 * channels]) for w in (0, 1)]
    vals = [spread(proj[w * 64 : w * 64 + 64, 2 * channels :]) for w in (0, 1)]
    raw = [dot(k, q, ((1,), (1,))) for k in keys]
    lane = lax.broadcasted_iota(jnp.int32, raw[0].shape, 1)
    scores = jnp.where(lane < 64, raw[0], raw[1]) * np.float32(1.0 / math.sqrt(depth))
    scores = scores.reshape(64, WIN, 128) + bias[...].reshape(64, WIN, 128)
    raised = jnp.exp(scores - jnp.max(scores, axis=0, keepdims=True))
    weights = raised * (1.0 / jnp.sum(raised, axis=0, keepdims=True))
    weights = jnp.transpose(weights.reshape(512, 128)).astype(BF16)
    heads = jnp.concatenate([dot(weights[w * 64 : w * 64 + 64], vals[w]) for w in (0, 1)], 0)
    return rounded(x + dot(heads.astype(BF16), merge))


def conv_phase(at_top, at_end, got, gain, expand, taps, shrink, tokens, normed, acc):
    lanes = got.shape[0]
    lane = lax.broadcasted_iota(jnp.int32, (400, 128), 1)
    row = lax.broadcasted_iota(jnp.int32, (400, 128), 0)
    lowest = jnp.where(at_top, 40, 0)
    highest = jnp.where(at_end, 360, 400)
    keep = (row >= lowest) & (row < highest)
    for i in range(0, lanes, 2):
        a = jnp.where(keep, got[i].astype(F32).reshape(400, 128), 0.0)
        b = jnp.where(keep, got[i + 1].astype(F32).reshape(400, 128), 0.0)
        cols = slice(i * HALF, i * HALF + 128)
        tokens[:400, cols] = jnp.where(lane < HALF, a, swapped(b))
        tokens[400:, cols] = jnp.where(lane < HALF, swapped(a), b)
    for half in (0, 1):
        normed[half * 400 : half * 400 + 400] = norm(
            tokens[half * 400 : half * 400 + 400], gain[...]
        )
    for half in (0, 1):
        for y in range(WIN):
            base = half * 400 + (y + 1) * 40
            acc[half * 256 + y * 32 : half * 256 + y * 32 + 32] = tokens[base : base + 32]

    width = min(512, expand.shape[1])
    inner = lax.broadcasted_iota(jnp.int32, (WIN, WIN, width), 1)

    def chunk(n, _):
        at = pl.ds(pl.multiple_of(n * width, width), width)
        kernel = taps[:, :, at].astype(F32) * 0.5
        for half in (0, 1):
            wide = twice_gelu(dot(normed[half * 400 : half * 400 + 400], expand[:, at]))
            wide = wide.reshape(10, 5, 8, width)

            def column(v, tile):
                total = None
                for u in range(3):
                    term = wide[u : u + WIN, tile] * kernel[u, v][None, None, :]
                    total = term if total is None else total + term
                return total

            left_rim, right_rim = column(0, 4), column(2, 4)
            parts = []
            for b in range(4):
                left = jnp.where(
                    inner == 0, left_rim[:, b : b + 1], pltpu.roll(column(0, b), 1, 1)
                )
                right = jnp.where(
                    inner == 7, right_rim[:, 4 + b : 5 + b], pltpu.roll(column(2, b), 7, 1)
                )
                parts.append(column(1, b) + left + right)
            summed = jnp.stack(parts, axis=1).reshape(256, width)
            narrow = dot(twice_gelu(summed).astype(BF16), shrink[at, :])
            acc[half * 256 : half * 256 + 256] += 0.5 * narrow
        return _

    lax.fori_loop(0, expand.shape[1] // width, chunk, 0)


def window_pair(n, gain, qkv, merge, bias, acc, done, send):
    channels = acc.shape[1]
    groups = []
    for w in (0, 1):
        b = n * 2 + w
        base = (b >> 2) * 256 + (b & 3) * 8
        groups += [acc[pl.ds(pl.multiple_of(base + y * 32, 8), 8)] for y in range(WIN)]
    x = rounded(jnp.concatenate(groups, 0))
    out = attend_pair(x, gain[...], qkv[...], merge[...], bias)
    for c in range(channels // 128):
        cols = slice(c * 128, c * 128 + 128)
        done[c] = out[:, cols]
        for x in range(WIN):
            send[x, n, :, cols] = done[c, pl.ds(x, 16, stride=8)].astype(BF16)


def group_pair(n, gain, qkv, merge, bias, mlp_gain, up, down, tokens, send):
    parts = tokens.shape[0]
    lane = lax.broadcasted_iota(jnp.int32, (64, 128), 1)
    halves = [
        jnp.concatenate([tokens[c, pl.ds(n + w * 4, 64, stride=8)] for c in range(parts)], 1)
        for w in (0, 1)
    ]
    x = attend_pair(jnp.concatenate(halves, 0), gain[...], qkv[...], merge[...], bias)
    hidden = twice_gelu(dot(norm(x, mlp_gain[...]), up[...])).astype(BF16)
    out = rounded(x + 0.5 * dot(hidden, down[...]))
    for c in range(parts):
        low, high = out[:64, c * 128 : c * 128 + 128], out[64:, c * 128 : c * 128 + 128]
        even = jnp.where(lane < HALF, low, swapped(high))
        odd = jnp.where(lane < HALF, swapped(low), high)
        send[:, 2 * c, n] = even.reshape(WIN, WIN, 128).astype(BF16)
        send[:, 2 * c + 1, n] = odd.reshape(WIN, WIN, 128).astype(BF16)


def finish_chunk(n, got, rows, out):
    lanes = got.shape[1]
    for x in range(WIN):
        for j in range(lanes):
            rows[pl.ds(j * 8 + x, 8, stride=8 * lanes)] = got[x, j, n].astype(F32)
    flat = jnp.transpose(rows[...]).astype(BF16)
    out[n] = flat[:HALF]
    out[n + 4] = flat[HALF:]


def whole_body(
    bands, lanes,
    px, first, second, mask, conv_gain, taps, block_gain, block_table,
    grid_gain, grid_table, mlp_gain,
    expand_far, shrink_far, block_qkv_far, block_merge_far,
    grid_qkv_far, grid_merge_far, up_far, down_far,
    out,
    expand, shrink, block_qkv, block_merge, grid_qkv, grid_merge, up, down, loaded,
    plane, send0, got0, tokens, normed, acc, flat, block_bias, grid_bias, done,
    send1, got1, columns, send2, got2, rows,
    ss0, rs0, os0, ss1, rs1, os1, ss2, rs2, os2,
):
    band, lane = lax.axis_index("rows"), lax.axis_index("ch")
    step = bands // WIN
    slot, rest = band // step, lax.rem(band, step)
    below, above = lax.rem(band + 1, bands), lax.rem(band + bands - 1, bands)
    lane_at = [lax.rem(lane + d, lanes) for d in range(lanes)]
    slot_at = [lax.rem(slot + d, WIN) for d in range(WIN)]
    band_at = [s * step + rest for s in slot_at]
    pairs = [(d, e) for d in range(WIN) for e in range(lanes) if d or e]
    barrier = pltpu.get_barrier_semaphore()
    partners = [(row, j) for row in (below, above) for j in lane_at]
    partners += [(band_at[d], lane_at[e]) for d, e in pairs]
    for partner in partners:
        pl.semaphore_signal(barrier, inc=1, device_id=partner, device_id_type=MESH)
    far = (
        expand_far, shrink_far, block_qkv_far, block_merge_far,
        grid_qkv_far, grid_merge_far, up_far, down_far,
    )
    near = (expand, shrink, block_qkv, block_merge, grid_qkv, grid_merge, up, down)
    loads = [
        pltpu.make_async_copy(f, m, loaded.at[i]) for i, (f, m) in enumerate(zip(far, near))
    ]
    for load in loads:
        load.start()
    prep_body(px, first, second, mask, plane, send0)
    pl.semaphore_wait(barrier, len(partners))

    def spread(kind, d, mine):
        row = (band, below, above)[kind]
        if kind == 0:
            src, dst = send0.at[lane_at[d]], got0.at[mine, pl.ds(1, WIN)]
        else:
            src = send0.at[lane_at[d], WIN - 1 if kind == 1 else 0]
            dst = got0.at[mine, 0 if kind == 1 else WIN + 1]
        return pltpu.make_async_remote_copy(
            src_ref=src, dst_ref=dst, send_sem=ss0.at[kind, d], recv_sem=rs0.at[kind, mine],
            device_id=(row, lane_at[d]), device_id_type=MESH,
        )

    spreads = [(k, d) for k in range(3) for d in range(lanes) if k or d]
    for k, d in spreads:
        spread(k, d, lane).start()
    own = pltpu.make_async_copy(send0.at[lane], got0.at[lane, pl.ds(1, WIN)], os0)
    own.start()
    bias_fill(block_table, flat, block_bias)
    bias_fill(grid_table, flat, grid_bias)
    own.wait()
    for load in loads:
        load.wait()
    for k, d in spreads:
        spread(k, d, lane_at[d]).wait_recv()
    conv_phase(
        band == 0, band == bands - 1, got0, conv_gain, expand, taps, shrink, tokens, normed, acc
    )

    def regroup(n, d, mine):
        return pltpu.make_async_remote_copy(
            src_ref=send1.at[slot_at[d], n], dst_ref=got1.at[mine, n],
            send_sem=ss1.at[n, d], recv_sem=rs1.at[n, mine],
            device_id=(band_at[d], lane), device_id_type=MESH,
        )

    def regroup_own(n):
        return pltpu.make_async_copy(send1.at[slot, n], got1.at[slot, n], os1.at[n])

    def windows(n, _):
        window_pair(n, block_gain, block_qkv, block_merge, block_bias, acc, done, send1)
        for d in range(1, WIN):
            regroup(n, d, slot).start()
        regroup_own(n).start()
        return _

    lax.fori_loop(0, 4, windows, 0)

    def arrive(n, _):
        regroup_own(n).wait()
        for d in range(1, WIN):
            regroup(n, d, slot_at[d]).wait_recv()
        for a in range(WIN):
            part = got1[a, n].astype(F32)
            for c in range(columns.shape[0]):
                columns[c, pl.ds(pl.multiple_of(a * 64 + n * 16, 16), 16)] = part[
                    :, c * 128 : c * 128 + 128
                ]
        return _

    lax.fori_loop(0, 4, arrive, 0)

    def home(n, d, e, from_slot, from_lane):
        return pltpu.make_async_remote_copy(
            src_ref=send2.at[slot_at[d], lane_at[e], n], dst_ref=got2.at[from_slot, from_lane, n],
            send_sem=ss2.at[n, d, e], recv_sem=rs2.at[n, from_slot, from_lane],
            device_id=(band_at[d], lane_at[e]), device_id_type=MESH,
        )

    def home_own(n):
        return pltpu.make_async_copy(
            send2.at[slot, lane, n], got2.at[slot, lane, n], os2.at[n]
        )

    def groups(n, _):
        group_pair(
            n, grid_gain, grid_qkv, grid_merge, grid_bias, mlp_gain, up, down, columns, send2
        )
        for d, e in pairs:
            home(n, d, e, slot, lane).start()
        home_own(n).start()
        return _

    lax.fori_loop(0, 4, groups, 0)

    def finish(n, _):
        home_own(n).wait()
        for d, e in pairs:
            home(n, d, e, slot_at[d], lane_at[e]).wait_recv()
        finish_chunk(n, got2, rows, out)
        return _

    lax.fori_loop(0, 4, finish, 0)
    for k, d in spreads:
        spread(k, d, lane).wait_send()

    def sent(n, _):
        for d in range(1, WIN):
            regroup(n, d, slot).wait_send()
        for d, e in pairs:
            home(n, d, e, slot, lane).wait_send()
        return _

    lax.fori_loop(0, 4, sent, 0)


def shards(
    pixels, conv_gain, expand_weight, depth_kernel, shrink_weight,
    block_gain, block_qkv, block_merge, block_bias,
    grid_gain, grid_qkv, grid_merge, grid_bias, mlp_gain, mlp_up, mlp_down,
):
    lanes, bands = lax.axis_size("ch"), lax.axis_size("rows")
    channels = expand_weight.shape[0]
    columns = pixels.shape[2]
    first, second, mask = pick_rows(lanes)
    operands = [
        pixels,
        jnp.asarray(first, BF16), jnp.asarray(second, BF16), jnp.asarray(mask, F32),
        conv_gain[None], depth_kernel,
        block_gain[None], jnp.transpose(block_bias, (1, 0, 2)),
        grid_gain[None], jnp.transpose(grid_bias, (1, 0, 2)), mlp_gain[None],
    ]
    weights = [
        expand_weight, shrink_weight, block_qkv, block_merge,
        grid_qkv, grid_merge, mlp_up, mlp_down,
    ]
    dma = pltpu.SemaphoreType.DMA
    out = pl.pallas_call(
        functools.partial(whole_body, bands, lanes),
        out_shape=jax.ShapeDtypeStruct((WIN, HALF, columns), BF16),
        in_specs=[VM] * len(operands) + [pl.BlockSpec(memory_space=pl.ANY)] * len(weights),
        out_specs=VM,
        scratch_shapes=[pltpu.VMEM(w.shape, w.dtype) for w in weights]
        + [
            dma((len(weights),)),
            pltpu.VMEM((columns // 128, HALF * WIN, 128), F32),
            pltpu.VMEM((lanes, WIN, 40, 128), BF16),
            pltpu.VMEM((lanes, WIN + 2, 40, 128), BF16),
            pltpu.VMEM((800, channels), F32),
            pltpu.VMEM((800, channels), BF16),
            pltpu.VMEM((512, channels), F32),
            pltpu.VMEM((WIN, 256), F32),
            pltpu.VMEM((WIN, WIN, WIN, 128), F32),
            pltpu.VMEM((WIN, WIN, WIN, 128), F32),
            pltpu.VMEM((channels // 128, 128, 128), F32),
            pltpu.VMEM((WIN, 4, 16, channels), BF16),
            pltpu.VMEM((WIN, 4, 16, channels), BF16),
            pltpu.VMEM((channels // 128, 512, 128), F32),
            pltpu.VMEM((WIN, lanes, 4, WIN, 128), BF16),
            pltpu.VMEM((WIN, lanes, 4, WIN, 128), BF16),
            pltpu.VMEM((columns, 128), F32),
            dma((3, lanes)), dma((3, lanes)), dma,
            dma((4, WIN)), dma((4, WIN)), dma((4,)),
            dma((4, WIN, lanes)), dma((4, WIN, lanes)), dma((4,)),
        ],
        compiler_params=pltpu.CompilerParams(
            collective_id=1, has_side_effects=True, vmem_limit_bytes=LIMIT
        ),
        name="maxvit",
    )(*operands, *weights)
    return jnp.transpose(out, (1, 0, 2))


def solution(mesh):
    in_specs = (P("ch", "rows", None),) + (P(),) * 15
    return jax.shard_map(
        shards, mesh=mesh, in_specs=in_specs, out_specs=P("ch", "rows", None), check_vma=False
    )
```

```python
import functools
import math

import jax
import jax.numpy as jnp
import numpy as np
from jax import lax
from jax.experimental import pallas as pl
from jax.experimental.pallas import tpu as pltpu
from jax.sharding import PartitionSpec as P

WIN = 8
HALF = 64
EPS = 1e-05
F32 = jnp.float32
BF16 = jnp.bfloat16
MESH = pl.DeviceIdType.MESH
VM = pl.BlockSpec(memory_space=pltpu.VMEM)
LIMIT = 56 * 1024 * 1024


def dot(a, b, dims=((1,), (0,))):
    return lax.dot_general(a, b, (dims, ((), ())), preferred_element_type=F32)


def norm(values, gain):
    middle = jnp.mean(values, axis=-1, keepdims=True)
    off = values - middle
    spread = jnp.mean(off * off, axis=-1, keepdims=True)
    return (off * lax.rsqrt(spread + EPS) * gain).astype(BF16)


def twice_gelu(v):
    return v * (1.0 + lax.erf(v * np.float32(math.sqrt(0.5))))


def rounded(v):
    return v.astype(BF16).astype(F32)


def swapped(v):
    return pltpu.roll(v, HALF, 1)


def pick_rows(lanes):
    width = 4 * lanes * WIN
    first = np.zeros((lanes * 40, width), np.float32)
    second = np.zeros((lanes * 40, width), np.float32)
    mask = np.zeros((lanes * 40, 128), np.float32)
    for j in range(lanes):
        for q in range(40):
            if q < 32:
                col = (q // 8 * lanes + j) * 8 + q % 8
            else:
                col = ((q - 32) % 4 * lanes + j) * 8 + (-1 if q < 36 else 8)
            row = j * 40 + q
            if col < 0:
                second[row, width - 1] = 1
                mask[row, HALF:] = 1
            elif col >= width:
                second[row, 0] = 1
                mask[row, :HALF] = 1
            else:
                first[row, col] = 1
    return first, second, mask


def prep_body(px, first, second, mask, plane, send):
    half = px.shape[2] // 2
    lanes = send.shape[0]
    for c in range(plane.shape[0]):
        part = px[:, :, c * 128 : c * 128 + 128].astype(F32)
        plane[c] = part.reshape(HALF * WIN, 128)
    for y in range(WIN):
        line = [plane[c, pl.ds(y, HALF, stride=WIN)] for c in range(plane.shape[0])]
        line = jnp.concatenate(line, 1).astype(BF16)
        low, high = line[:, :half], line[:, half:]
        main = dot(first[...], jnp.concatenate([low, high], 0), ((1,), (1,)))
        rim = dot(second[...], jnp.concatenate([high, low], 0), ((1,), (1,)))
        rows = (main + rim * mask[...]).astype(BF16)
        for j in range(lanes):
            send[j, y] = rows[j * 40 : (j + 1) * 40]


def bias_fill(table, flat, bias):
    flat[...] = jnp.zeros_like(flat)
    for i in range(2 * WIN - 1):
        flat[:, i * 16 : i * 16 + 15] = table[i]
    t = flat[...]
    shifted = [t if z == 0 else pltpu.roll(t, 256 - z * 16, 1) for z in range(WIN)]
    rows = jnp.concatenate([s[:, :128] for s in shifted], 0)
    r = lax.broadcasted_iota(jnp.int32, (128, 128), 0)
    c = lax.broadcasted_iota(jnp.int32, (128, 128), 1)
    m, j = r >> 4, r & 15
    y, x = (c >> 3) & 7, c & 7
    for v in range(WIN):
        onehot = jnp.where((m == 7 - y) & (j == v - x + 7), 1.0, 0.0).astype(F32)
        got = lax.dot_general(
            rows, onehot, (((1,), (0,)), ((), ())),
            precision=lax.Precision.HIGHEST, preferred_element_type=F32,
        )
        for z in range(WIN):
            bias[pl.ds(z * 8 + v, WIN, stride=64)] = got[z * 8 : z * 8 + 8]


def attend_pair(x, gain, qkv, merge, bias):
    channels = x.shape[1]
    depth = channels // WIN
    proj = dot(norm(x, gain), qkv)
    q = proj[:, :channels].astype(BF16)
    place = lax.broadcasted_iota(jnp.int32, (1, channels), 1)
    own = [
        jnp.where((place >= h * depth) & (place < h * depth + depth), 1.0, 0.0).astype(BF16)
        for h in range(WIN)
    ]

    def spread(rows):
        rows = rows.astype(BF16)
        return jnp.concatenate([rows * o for o in own], 0)

    keys = [spread(proj[w * 64 : w * 64 + 64, channels : 2 * channels]) for w in (0, 1)]
    vals = [spread(proj[w * 64 : w * 64 + 64, 2 * channels :]) for w in (0, 1)]
    raw = [dot(k, q, ((1,), (1,))) for k in keys]
    lane = lax.broadcasted_iota(jnp.int32, raw[0].shape, 1)
    scores = jnp.where(lane < 64, raw[0], raw[1]) * np.float32(1.0 / math.sqrt(depth))
    scores = (scores + bias[...]).reshape(WIN, 64, 128)
    raised = jnp.exp(scores - jnp.max(scores, axis=1, keepdims=True))
    weights = raised * (1.0 / jnp.sum(raised, axis=1, keepdims=True))
    weights = jnp.transpose(weights.reshape(512, 128)).astype(BF16)
    heads = jnp.concatenate([dot(weights[w * 64 : w * 64 + 64], vals[w]) for w in (0, 1)], 0)
    return rounded(x + dot(heads.astype(BF16), merge))


def conv_phase(at_top, at_end, got, gain, expand, taps, shrink, tokens, normed, acc):
    lanes = got.shape[0]
    lane = lax.broadcasted_iota(jnp.int32, (400, 128), 1)
    row = lax.broadcasted_iota(jnp.int32, (400, 128), 0)
    lowest = jnp.where(at_top, 40, 0)
    highest = jnp.where(at_end, 360, 400)
    keep = (row >= lowest) & (row < highest)
    for i in range(0, lanes, 2):
        a = jnp.where(keep, got[i].astype(F32).reshape(400, 128), 0.0)
        b = jnp.where(keep, got[i + 1].astype(F32).reshape(400, 128), 0.0)
        cols = slice(i * HALF, i * HALF + 128)
        tokens[:400, cols] = jnp.where(lane < HALF, a, swapped(b))
        tokens[400:, cols] = jnp.where(lane < HALF, swapped(a), b)
    for half in (0, 1):
        normed[half * 400 : half * 400 + 400] = norm(
            tokens[half * 400 : half * 400 + 400], gain[...]
        )
    for half in (0, 1):
        for y in range(WIN):
            base = half * 400 + (y + 1) * 40
            acc[half * 256 + y * 32 : half * 256 + y * 32 + 32] = tokens[base : base + 32]

    width = min(512, expand.shape[1])
    inner = lax.broadcasted_iota(jnp.int32, (WIN, WIN, width), 1)

    def chunk(n, _):
        at = pl.ds(pl.multiple_of(n * width, width), width)
        kernel = taps[:, :, at].astype(F32) * 0.5
        for half in (0, 1):
            wide = twice_gelu(dot(normed[half * 400 : half * 400 + 400], expand[:, at]))
            wide = wide.reshape(10, 5, 8, width)

            def column(v, tile):
                total = None
                for u in range(3):
                    term = wide[u : u + WIN, tile] * kernel[u, v][None, None, :]
                    total = term if total is None else total + term
                return total

            left_rim, right_rim = column(0, 4), column(2, 4)
            parts = []
            for b in range(4):
                left = jnp.where(
                    inner == 0, left_rim[:, b : b + 1], pltpu.roll(column(0, b), 1, 1)
                )
                right = jnp.where(
                    inner == 7, right_rim[:, 4 + b : 5 + b], pltpu.roll(column(2, b), 7, 1)
                )
                parts.append(column(1, b) + left + right)
            summed = jnp.stack(parts, axis=1).reshape(256, width)
            narrow = dot(twice_gelu(summed).astype(BF16), shrink[at, :])
            acc[half * 256 : half * 256 + 256] += 0.5 * narrow
        return _

    lax.fori_loop(0, expand.shape[1] // width, chunk, 0)


def window_pair(n, gain, qkv, merge, bias, acc, done, send):
    channels = acc.shape[1]
    groups = []
    for w in (0, 1):
        b = n * 2 + w
        base = (b >> 2) * 256 + (b & 3) * 8
        groups += [acc[pl.ds(pl.multiple_of(base + y * 32, 8), 8)] for y in range(WIN)]
    x = rounded(jnp.concatenate(groups, 0))
    out = attend_pair(x, gain[...], qkv[...], merge[...], bias)
    for c in range(channels // 128):
        cols = slice(c * 128, c * 128 + 128)
        done[c] = out[:, cols]
        for x in range(WIN):
            send[x, n, :, cols] = done[c, pl.ds(x, 16, stride=8)].astype(BF16)


def group_pair(n, gain, qkv, merge, bias, mlp_gain, up, down, tokens, send):
    parts = tokens.shape[0]
    lane = lax.broadcasted_iota(jnp.int32, (64, 128), 1)
    halves = [
        jnp.concatenate([tokens[c, pl.ds(n + w * 4, 64, stride=8)] for c in range(parts)], 1)
        for w in (0, 1)
    ]
    x = attend_pair(jnp.concatenate(halves, 0), gain[...], qkv[...], merge[...], bias)
    hidden = twice_gelu(dot(norm(x, mlp_gain[...]), up[...])).astype(BF16)
    out = rounded(x + 0.5 * dot(hidden, down[...]))
    for c in range(parts):
        low, high = out[:64, c * 128 : c * 128 + 128], out[64:, c * 128 : c * 128 + 128]
        even = jnp.where(lane < HALF, low, swapped(high))
        odd = jnp.where(lane < HALF, swapped(low), high)
        send[:, 2 * c, n] = even.reshape(WIN, WIN, 128).astype(BF16)
        send[:, 2 * c + 1, n] = odd.reshape(WIN, WIN, 128).astype(BF16)


def finish_chunk(n, got, rows, plane):
    lanes = got.shape[1]
    for x in range(WIN):
        for j in range(lanes):
            rows[pl.ds(j * 8 + x, 8, stride=8 * lanes)] = got[x, j, n].astype(F32)
    for c in range(plane.shape[0]):
        flat = jnp.transpose(rows[c * 128 : c * 128 + 128])
        plane[c, pl.ds(n, HALF, stride=WIN)] = flat[:HALF]
        plane[c, pl.ds(n + 4, HALF, stride=WIN)] = flat[HALF:]


def whole_body(
    bands, lanes,
    px, first, second, mask, conv_gain, taps, block_gain, block_table,
    grid_gain, grid_table, mlp_gain,
    expand_far, shrink_far, block_qkv_far, block_merge_far,
    grid_qkv_far, grid_merge_far, up_far, down_far,
    out,
    expand, shrink, block_qkv, block_merge, grid_qkv, grid_merge, up, down, loaded,
    plane, send0, got0, tokens, normed, acc, flat, block_bias, grid_bias, done,
    send1, got1, columns, send2, got2, rows,
    ss0, rs0, os0, ss1, rs1, os1, ss2, rs2, os2,
):
    band, lane = lax.axis_index("rows"), lax.axis_index("ch")
    step = bands // WIN
    slot, rest = band // step, lax.rem(band, step)
    below, above = lax.rem(band + 1, bands), lax.rem(band + bands - 1, bands)
    lane_at = [lax.rem(lane + d, lanes) for d in range(lanes)]
    slot_at = [lax.rem(slot + d, WIN) for d in range(WIN)]
    band_at = [s * step + rest for s in slot_at]
    pairs = [(d, e) for d in range(WIN) for e in range(lanes) if d or e]
    barrier = pltpu.get_barrier_semaphore()
    partners = [(row, j) for row in (below, above) for j in lane_at]
    partners += [(band_at[d], lane_at[e]) for d, e in pairs]
    for partner in partners:
        pl.semaphore_signal(barrier, inc=1, device_id=partner, device_id_type=MESH)
    far = (
        expand_far, shrink_far, block_qkv_far, block_merge_far,
        grid_qkv_far, grid_merge_far, up_far, down_far,
    )
    near = (expand, shrink, block_qkv, block_merge, grid_qkv, grid_merge, up, down)
    loads = [
        pltpu.make_async_copy(f, m, loaded.at[i]) for i, (f, m) in enumerate(zip(far, near))
    ]
    for load in loads:
        load.start()
    prep_body(px, first, second, mask, plane, send0)
    pl.semaphore_wait(barrier, len(partners))

    def spread(kind, d, mine):
        row = (band, below, above)[kind]
        if kind == 0:
            src, dst = send0.at[lane_at[d]], got0.at[mine, pl.ds(1, WIN)]
        else:
            src = send0.at[lane_at[d], WIN - 1 if kind == 1 else 0]
            dst = got0.at[mine, 0 if kind == 1 else WIN + 1]
        return pltpu.make_async_remote_copy(
            src_ref=src, dst_ref=dst, send_sem=ss0.at[kind, d], recv_sem=rs0.at[kind, mine],
            device_id=(row, lane_at[d]), device_id_type=MESH,
        )

    spreads = [(k, d) for k in range(3) for d in range(lanes) if k or d]
    for k, d in spreads:
        spread(k, d, lane).start()
    own = pltpu.make_async_copy(send0.at[lane], got0.at[lane, pl.ds(1, WIN)], os0)
    own.start()
    bias_fill(block_table, flat, block_bias)
    bias_fill(grid_table, flat, grid_bias)
    own.wait()
    for load in loads:
        load.wait()
    for k, d in spreads:
        spread(k, d, lane_at[d]).wait_recv()
    conv_phase(
        band == 0, band == bands - 1, got0, conv_gain, expand, taps, shrink, tokens, normed, acc
    )

    def regroup(n, d, mine):
        return pltpu.make_async_remote_copy(
            src_ref=send1.at[slot_at[d], n], dst_ref=got1.at[mine, n],
            send_sem=ss1.at[n, d], recv_sem=rs1.at[n, mine],
            device_id=(band_at[d], lane), device_id_type=MESH,
        )

    def regroup_own(n):
        return pltpu.make_async_copy(send1.at[slot, n], got1.at[slot, n], os1.at[n])

    def windows(n, _):
        window_pair(n, block_gain, block_qkv, block_merge, block_bias, acc, done, send1)
        for d in range(1, WIN):
            regroup(n, d, slot).start()
        regroup_own(n).start()
        return _

    lax.fori_loop(0, 4, windows, 0)

    def arrive(n, _):
        regroup_own(n).wait()
        for d in range(1, WIN):
            regroup(n, d, slot_at[d]).wait_recv()
        for a in range(WIN):
            part = got1[a, n].astype(F32)
            for c in range(columns.shape[0]):
                columns[c, pl.ds(pl.multiple_of(a * 64 + n * 16, 16), 16)] = part[
                    :, c * 128 : c * 128 + 128
                ]
        return _

    lax.fori_loop(0, 4, arrive, 0)

    def home(n, d, e, from_slot, from_lane):
        return pltpu.make_async_remote_copy(
            src_ref=send2.at[slot_at[d], lane_at[e], n], dst_ref=got2.at[from_slot, from_lane, n],
            send_sem=ss2.at[n, d, e], recv_sem=rs2.at[n, from_slot, from_lane],
            device_id=(band_at[d], lane_at[e]), device_id_type=MESH,
        )

    def home_own(n):
        return pltpu.make_async_copy(
            send2.at[slot, lane, n], got2.at[slot, lane, n], os2.at[n]
        )

    def groups(n, _):
        group_pair(
            n, grid_gain, grid_qkv, grid_merge, grid_bias, mlp_gain, up, down, columns, send2
        )
        for d, e in pairs:
            home(n, d, e, slot, lane).start()
        home_own(n).start()
        return _

    lax.fori_loop(0, 4, groups, 0)

    def finish(n, _):
        home_own(n).wait()
        for d, e in pairs:
            home(n, d, e, slot_at[d], lane_at[e]).wait_recv()
        finish_chunk(n, got2, rows, plane)
        return _

    lax.fori_loop(0, 4, finish, 0)
    for c in range(plane.shape[0]):
        out[:, :, c * 128 : c * 128 + 128] = plane[c].reshape(HALF, WIN, 128).astype(BF16)
    for k, d in spreads:
        spread(k, d, lane).wait_send()

    def sent(n, _):
        for d in range(1, WIN):
            regroup(n, d, slot).wait_send()
        for d, e in pairs:
            home(n, d, e, slot, lane).wait_send()
        return _

    lax.fori_loop(0, 4, sent, 0)


def shards(
    pixels, conv_gain, expand_weight, depth_kernel, shrink_weight,
    block_gain, block_qkv, block_merge, block_bias,
    grid_gain, grid_qkv, grid_merge, grid_bias, mlp_gain, mlp_up, mlp_down,
):
    lanes, bands = lax.axis_size("ch"), lax.axis_size("rows")
    channels = expand_weight.shape[0]
    columns = pixels.shape[2]
    first, second, mask = pick_rows(lanes)
    operands = [
        pixels,
        jnp.asarray(first, BF16), jnp.asarray(second, BF16), jnp.asarray(mask, F32),
        conv_gain[None], depth_kernel,
        block_gain[None], jnp.transpose(block_bias, (1, 0, 2)),
        grid_gain[None], jnp.transpose(grid_bias, (1, 0, 2)), mlp_gain[None],
    ]
    weights = [
        expand_weight, shrink_weight, block_qkv, block_merge,
        grid_qkv, grid_merge, mlp_up, mlp_down,
    ]
    dma = pltpu.SemaphoreType.DMA
    return pl.pallas_call(
        functools.partial(whole_body, bands, lanes),
        out_shape=jax.ShapeDtypeStruct((HALF, WIN, columns), BF16),
        in_specs=[VM] * len(operands) + [pl.BlockSpec(memory_space=pl.ANY)] * len(weights),
        out_specs=VM,
        scratch_shapes=[pltpu.VMEM(w.shape, w.dtype) for w in weights]
        + [
            dma((len(weights),)),
            pltpu.VMEM((columns // 128, HALF * WIN, 128), F32),
            pltpu.VMEM((lanes, WIN, 40, 128), BF16),
            pltpu.VMEM((lanes, WIN + 2, 40, 128), BF16),
            pltpu.VMEM((800, channels), F32),
            pltpu.VMEM((800, channels), BF16),
            pltpu.VMEM((512, channels), F32),
            pltpu.VMEM((WIN, 256), F32),
            pltpu.VMEM((512, 128), F32),
            pltpu.VMEM((512, 128), F32),
            pltpu.VMEM((channels // 128, 128, 128), F32),
            pltpu.VMEM((WIN, 4, 16, channels), BF16),
            pltpu.VMEM((WIN, 4, 16, channels), BF16),
            pltpu.VMEM((channels // 128, 512, 128), F32),
            pltpu.VMEM((WIN, lanes, 4, WIN, 128), BF16),
            pltpu.VMEM((WIN, lanes, 4, WIN, 128), BF16),
            pltpu.VMEM((columns, 128), F32),
            dma((3, lanes)), dma((3, lanes)), dma,
            dma((4, WIN)), dma((4, WIN)), dma((4,)),
            dma((4, WIN, lanes)), dma((4, WIN, lanes)), dma((4,)),
        ],
        compiler_params=pltpu.CompilerParams(
            collective_id=1, has_side_effects=True, vmem_limit_bytes=LIMIT
        ),
        name="maxvit",
    )(*operands, *weights)


def solution(mesh):
    in_specs = (P("ch", "rows", None),) + (P(),) * 15
    return jax.shard_map(
        shards, mesh=mesh, in_specs=in_specs, out_specs=P("ch", "rows", None), check_vma=False
    )
```

```python
import functools
import math

import jax
import jax.numpy as jnp
import numpy as np
from jax import lax
from jax.experimental import pallas as pl
from jax.experimental.pallas import tpu as pltpu
from jax.sharding import PartitionSpec as P

WIN = 8
HALF = 64
EPS = 1e-05
F32 = jnp.float32
BF16 = jnp.bfloat16
MESH = pl.DeviceIdType.MESH
VM = pl.BlockSpec(memory_space=pltpu.VMEM)
LIMIT = 56 * 1024 * 1024


def dot(a, b, dims=((1,), (0,))):
    return lax.dot_general(a, b, (dims, ((), ())), preferred_element_type=F32)


def norm(values, gain):
    middle = jnp.mean(values, axis=-1, keepdims=True)
    off = values - middle
    spread = jnp.mean(off * off, axis=-1, keepdims=True)
    return (off * lax.rsqrt(spread + EPS) * gain).astype(BF16)


def twice_gelu(v):
    return v * (1.0 + lax.erf(v * np.float32(math.sqrt(0.5))))


def rounded(v):
    return v.astype(BF16).astype(F32)


def swapped(v):
    return pltpu.roll(v, HALF, 1)


def pick_rows(lanes):
    width = 4 * lanes * WIN
    first = np.zeros((lanes * 40, width), np.float32)
    second = np.zeros((lanes * 40, width), np.float32)
    mask = np.zeros((lanes * 40, 128), np.float32)
    for j in range(lanes):
        for q in range(40):
            if q < 32:
                col = (q // 8 * lanes + j) * 8 + q % 8
            else:
                col = ((q - 32) % 4 * lanes + j) * 8 + (-1 if q < 36 else 8)
            row = j * 40 + q
            if col < 0:
                second[row, width - 1] = 1
                mask[row, HALF:] = 1
            elif col >= width:
                second[row, 0] = 1
                mask[row, :HALF] = 1
            else:
                first[row, col] = 1
    return first, second, mask


def prep_body(px, first, second, mask, plane, send):
    half = px.shape[2] // 2
    lanes = send.shape[0]
    for c in range(plane.shape[0]):
        part = px[:, :, c * 128 : c * 128 + 128].astype(F32)
        plane[c] = part.reshape(HALF * WIN, 128)
    for y in range(WIN):
        line = [plane[c, pl.ds(y, HALF, stride=WIN)] for c in range(plane.shape[0])]
        line = jnp.concatenate(line, 1).astype(BF16)
        low, high = line[:, :half], line[:, half:]
        main = dot(first[...], jnp.concatenate([low, high], 0), ((1,), (1,)))
        rim = dot(second[...], jnp.concatenate([high, low], 0), ((1,), (1,)))
        rows = (main + rim * mask[...]).astype(BF16)
        for j in range(lanes):
            send[j, y] = rows[j * 40 : (j + 1) * 40]


def bias_fill(table, flat, bias):
    flat[...] = jnp.zeros_like(flat)
    for i in range(2 * WIN - 1):
        flat[:, i * 16 : i * 16 + 15] = table[i]
    t = flat[...]
    shifted = [t if z == 0 else pltpu.roll(t, 256 - z * 16, 1) for z in range(WIN)]
    rows = jnp.concatenate([s[:, :128] for s in shifted], 0)
    r = lax.broadcasted_iota(jnp.int32, (128, 128), 0)
    c = lax.broadcasted_iota(jnp.int32, (128, 128), 1)
    m, j = r >> 4, r & 15
    y, x = (c >> 3) & 7, c & 7
    for v in range(WIN):
        onehot = jnp.where((m == 7 - y) & (j == v - x + 7), 1.0, 0.0).astype(F32)
        got = lax.dot_general(
            rows, onehot, (((1,), (0,)), ((), ())),
            precision=lax.Precision.HIGHEST, preferred_element_type=F32,
        )
        for z in range(WIN):
            bias[pl.ds(z * 8 + v, WIN, stride=64)] = got[z * 8 : z * 8 + 8]


def attend_pair(x, gain, qkv, merge, bias):
    channels = x.shape[1]
    depth = channels // WIN
    proj = dot(norm(x, gain), qkv)
    q = proj[:, :channels].astype(BF16)
    place = lax.broadcasted_iota(jnp.int32, (1, channels), 1)
    own = [
        jnp.where((place >= h * depth) & (place < h * depth + depth), 1.0, 0.0).astype(BF16)
        for h in range(WIN)
    ]

    def spread(rows):
        rows = rows.astype(BF16)
        return jnp.concatenate([rows * o for o in own], 0)

    keys = [spread(proj[w * 64 : w * 64 + 64, channels : 2 * channels]) for w in (0, 1)]
    vals = [spread(proj[w * 64 : w * 64 + 64, 2 * channels :]) for w in (0, 1)]
    raw = [dot(k, q, ((1,), (1,))) for k in keys]
    lane = lax.broadcasted_iota(jnp.int32, raw[0].shape, 1)
    scores = jnp.where(lane < 64, raw[0], raw[1]) * np.float32(1.0 / math.sqrt(depth))
    scores = (scores + bias[...]).reshape(WIN, 64, 128)
    raised = jnp.exp(scores - jnp.max(scores, axis=1, keepdims=True))
    weights = raised * (1.0 / jnp.sum(raised, axis=1, keepdims=True))
    weights = jnp.transpose(weights.reshape(512, 128)).astype(BF16)
    heads = jnp.concatenate([dot(weights[w * 64 : w * 64 + 64], vals[w]) for w in (0, 1)], 0)
    return rounded(x + dot(heads.astype(BF16), merge))


def conv_phase(part, at_edge, got, gain, expand, taps, shrink, tokens, normed, acc):
    lanes = got.shape[0]
    lane = lax.broadcasted_iota(jnp.int32, (240, 128), 1)
    row = lax.broadcasted_iota(jnp.int32, (240, 128), 0)
    if part == 0:
        keep = row >= jnp.where(at_edge, 40, 0)
    else:
        keep = row < jnp.where(at_edge, 200, 240)
    own_rows = slice(part * 4, part * 4 + 6)
    for i in range(0, lanes, 2):
        a = jnp.where(keep, got[i, own_rows].astype(F32).reshape(240, 128), 0.0)
        b = jnp.where(keep, got[i + 1, own_rows].astype(F32).reshape(240, 128), 0.0)
        cols = slice(i * HALF, i * HALF + 128)
        tokens[:240, cols] = jnp.where(lane < HALF, a, swapped(b))
        tokens[240:, cols] = jnp.where(lane < HALF, swapped(a), b)
    for half in (0, 1):
        normed[half * 240 : half * 240 + 240] = norm(
            tokens[half * 240 : half * 240 + 240], gain[...]
        )
    for half in (0, 1):
        for y in range(4):
            base = half * 240 + (y + 1) * 40
            at = half * 256 + part * 128 + y * 32
            acc[at : at + 32] = tokens[base : base + 32]

    width = min(512, expand.shape[1])
    inner = lax.broadcasted_iota(jnp.int32, (4, WIN, width), 1)

    def chunk(n, _):
        at = pl.ds(pl.multiple_of(n * width, width), width)
        kernel = taps[:, :, at].astype(F32) * 0.5
        for half in (0, 1):
            wide = twice_gelu(dot(normed[half * 240 : half * 240 + 240], expand[:, at]))
            wide = wide.reshape(6, 5, 8, width)

            def column(v, tile):
                total = None
                for u in range(3):
                    term = wide[u : u + 4, tile] * kernel[u, v][None, None, :]
                    total = term if total is None else total + term
                return total

            left_rim, right_rim = column(0, 4), column(2, 4)
            parts = []
            for b in range(4):
                left = jnp.where(
                    inner == 0, left_rim[:, b : b + 1], pltpu.roll(column(0, b), 1, 1)
                )
                right = jnp.where(
                    inner == 7, right_rim[:, 4 + b : 5 + b], pltpu.roll(column(2, b), 7, 1)
                )
                parts.append(column(1, b) + left + right)
            summed = jnp.stack(parts, axis=1).reshape(128, width)
            narrow = dot(twice_gelu(summed).astype(BF16), shrink[at, :])
            base = half * 256 + part * 128
            acc[base : base + 128] += 0.5 * narrow
        return _

    lax.fori_loop(0, expand.shape[1] // width, chunk, 0)


def window_pair(n, gain, qkv, merge, bias, acc, done, send):
    channels = acc.shape[1]
    groups = []
    for w in (0, 1):
        b = n * 2 + w
        base = (b >> 2) * 256 + (b & 3) * 8
        groups += [acc[pl.ds(pl.multiple_of(base + y * 32, 8), 8)] for y in range(WIN)]
    x = rounded(jnp.concatenate(groups, 0))
    out = attend_pair(x, gain[...], qkv[...], merge[...], bias)
    for c in range(channels // 128):
        cols = slice(c * 128, c * 128 + 128)
        done[c] = out[:, cols]
        for x in range(WIN):
            send[x, n, :, cols] = done[c, pl.ds(x, 16, stride=8)].astype(BF16)


def group_pair(n, gain, qkv, merge, bias, mlp_gain, up, down, tokens, send):
    parts = tokens.shape[0]
    lane = lax.broadcasted_iota(jnp.int32, (64, 128), 1)
    halves = [
        jnp.concatenate([tokens[c, pl.ds(n + w * 4, 64, stride=8)] for c in range(parts)], 1)
        for w in (0, 1)
    ]
    x = attend_pair(jnp.concatenate(halves, 0), gain[...], qkv[...], merge[...], bias)
    hidden = twice_gelu(dot(norm(x, mlp_gain[...]), up[...])).astype(BF16)
    out = rounded(x + 0.5 * dot(hidden, down[...]))
    for c in range(parts):
        low, high = out[:64, c * 128 : c * 128 + 128], out[64:, c * 128 : c * 128 + 128]
        even = jnp.where(lane < HALF, low, swapped(high))
        odd = jnp.where(lane < HALF, swapped(low), high)
        send[:, 2 * c, n] = even.reshape(WIN, WIN, 128).astype(BF16)
        send[:, 2 * c + 1, n] = odd.reshape(WIN, WIN, 128).astype(BF16)


def finish_chunk(n, got, rows, plane):
    lanes = got.shape[1]
    for x in range(WIN):
        for j in range(lanes):
            rows[pl.ds(j * 8 + x, 8, stride=8 * lanes)] = got[x, j, n].astype(F32)
    for c in range(plane.shape[0]):
        flat = jnp.transpose(rows[c * 128 : c * 128 + 128])
        plane[c, pl.ds(n, HALF, stride=WIN)] = flat[:HALF]
        plane[c, pl.ds(n + 4, HALF, stride=WIN)] = flat[HALF:]


def whole_body(
    bands, lanes,
    px, first, second, mask, conv_gain, taps, block_gain, block_table,
    grid_gain, grid_table, mlp_gain,
    expand_far, shrink_far, block_qkv_far, block_merge_far,
    grid_qkv_far, grid_merge_far, up_far, down_far,
    out,
    expand, shrink, block_qkv, block_merge, grid_qkv, grid_merge, up, down, loaded,
    plane, send0, got0, tokens, normed, acc, flat, block_bias, grid_bias, done,
    send1, got1, columns, send2, got2, rows,
    ss0, rs0, os0, ss1, rs1, os1, ss2, rs2, os2,
):
    band, lane = lax.axis_index("rows"), lax.axis_index("ch")
    step = bands // WIN
    slot, rest = band // step, lax.rem(band, step)
    below, above = lax.rem(band + 1, bands), lax.rem(band + bands - 1, bands)
    lane_at = [lax.rem(lane + d, lanes) for d in range(lanes)]
    slot_at = [lax.rem(slot + d, WIN) for d in range(WIN)]
    band_at = [s * step + rest for s in slot_at]
    pairs = [(d, e) for d in range(WIN) for e in range(lanes) if d or e]
    barrier = pltpu.get_barrier_semaphore()
    partners = [(row, j) for row in (below, above) for j in lane_at]
    partners += [(band_at[d], lane_at[e]) for d, e in pairs]
    for partner in partners:
        pl.semaphore_signal(barrier, inc=1, device_id=partner, device_id_type=MESH)
    far = (
        expand_far, shrink_far, block_qkv_far, block_merge_far,
        grid_qkv_far, grid_merge_far, up_far, down_far,
    )
    near = (expand, shrink, block_qkv, block_merge, grid_qkv, grid_merge, up, down)
    loads = [
        pltpu.make_async_copy(f, m, loaded.at[i]) for i, (f, m) in enumerate(zip(far, near))
    ]
    for load in loads:
        load.start()
    prep_body(px, first, second, mask, plane, send0)
    pl.semaphore_wait(barrier, len(partners))

    def spread(kind, d, mine):
        row = (band, below, above, band)[kind]
        if kind == 0:
            src, dst = send0.at[lane_at[d], pl.ds(0, 5)], got0.at[mine, pl.ds(1, 5)]
        elif kind == 3:
            src, dst = send0.at[lane_at[d], pl.ds(5, 3)], got0.at[mine, pl.ds(6, 3)]
        else:
            src = send0.at[lane_at[d], WIN - 1 if kind == 1 else 0]
            dst = got0.at[mine, 0 if kind == 1 else WIN + 1]
        return pltpu.make_async_remote_copy(
            src_ref=src, dst_ref=dst, send_sem=ss0.at[kind, d], recv_sem=rs0.at[kind, mine],
            device_id=(row, lane_at[d]), device_id_type=MESH,
        )

    spreads = [(k, d) for k in (0, 1, 3, 2) for d in range(lanes) if k % 3 or d]
    for k, d in spreads:
        spread(k, d, lane).start()
    own = pltpu.make_async_copy(send0.at[lane], got0.at[lane, pl.ds(1, WIN)], os0)
    own.start()
    bias_fill(block_table, flat, block_bias)
    bias_fill(grid_table, flat, grid_bias)
    own.wait()
    for load in loads:
        load.wait()
    for part in (0, 1):
        for k, d in spreads:
            if k // 2 == part:
                spread(k, d, lane_at[d]).wait_recv()
        at_edge = band == (0 if part == 0 else bands - 1)
        conv_phase(part, at_edge, got0, conv_gain, expand, taps, shrink, tokens, normed, acc)

    def regroup(n, d, mine):
        return pltpu.make_async_remote_copy(
            src_ref=send1.at[slot_at[d], n], dst_ref=got1.at[mine, n],
            send_sem=ss1.at[n, d], recv_sem=rs1.at[n, mine],
            device_id=(band_at[d], lane), device_id_type=MESH,
        )

    def regroup_own(n):
        return pltpu.make_async_copy(send1.at[slot, n], got1.at[slot, n], os1.at[n])

    def windows(n, _):
        window_pair(n, block_gain, block_qkv, block_merge, block_bias, acc, done, send1)
        for d in range(1, WIN):
            regroup(n, d, slot).start()
        regroup_own(n).start()
        return _

    lax.fori_loop(0, 4, windows, 0)

    def arrive(n, _):
        regroup_own(n).wait()
        for d in range(1, WIN):
            regroup(n, d, slot_at[d]).wait_recv()
        for a in range(WIN):
            part = got1[a, n].astype(F32)
            for c in range(columns.shape[0]):
                columns[c, pl.ds(pl.multiple_of(a * 64 + n * 16, 16), 16)] = part[
                    :, c * 128 : c * 128 + 128
                ]
        return _

    lax.fori_loop(0, 4, arrive, 0)

    def home(n, d, e, from_slot, from_lane):
        return pltpu.make_async_remote_copy(
            src_ref=send2.at[slot_at[d], lane_at[e], n], dst_ref=got2.at[from_slot, from_lane, n],
            send_sem=ss2.at[n, d, e], recv_sem=rs2.at[n, from_slot, from_lane],
            device_id=(band_at[d], lane_at[e]), device_id_type=MESH,
        )

    def home_own(n):
        return pltpu.make_async_copy(
            send2.at[slot, lane, n], got2.at[slot, lane, n], os2.at[n]
        )

    def groups(n, _):
        group_pair(
            n, grid_gain, grid_qkv, grid_merge, grid_bias, mlp_gain, up, down, columns, send2
        )
        for d, e in pairs:
            home(n, d, e, slot, lane).start()
        home_own(n).start()
        return _

    lax.fori_loop(0, 4, groups, 0)

    def finish(n, _):
        home_own(n).wait()
        for d, e in pairs:
            home(n, d, e, slot_at[d], lane_at[e]).wait_recv()
        finish_chunk(n, got2, rows, plane)
        return _

    lax.fori_loop(0, 4, finish, 0)
    for c in range(plane.shape[0]):
        out[:, :, c * 128 : c * 128 + 128] = plane[c].reshape(HALF, WIN, 128).astype(BF16)
    for k, d in spreads:
        spread(k, d, lane).wait_send()

    def sent(n, _):
        for d in range(1, WIN):
            regroup(n, d, slot).wait_send()
        for d, e in pairs:
            home(n, d, e, slot, lane).wait_send()
        return _

    lax.fori_loop(0, 4, sent, 0)


def shards(
    pixels, conv_gain, expand_weight, depth_kernel, shrink_weight,
    block_gain, block_qkv, block_merge, block_bias,
    grid_gain, grid_qkv, grid_merge, grid_bias, mlp_gain, mlp_up, mlp_down,
):
    lanes, bands = lax.axis_size("ch"), lax.axis_size("rows")
    channels = expand_weight.shape[0]
    columns = pixels.shape[2]
    first, second, mask = pick_rows(lanes)
    operands = [
        pixels,
        jnp.asarray(first, BF16), jnp.asarray(second, BF16), jnp.asarray(mask, F32),
        conv_gain[None], depth_kernel,
        block_gain[None], jnp.transpose(block_bias, (1, 0, 2)),
        grid_gain[None], jnp.transpose(grid_bias, (1, 0, 2)), mlp_gain[None],
    ]
    weights = [
        expand_weight, shrink_weight, block_qkv, block_merge,
        grid_qkv, grid_merge, mlp_up, mlp_down,
    ]
    dma = pltpu.SemaphoreType.DMA
    return pl.pallas_call(
        functools.partial(whole_body, bands, lanes),
        out_shape=jax.ShapeDtypeStruct((HALF, WIN, columns), BF16),
        in_specs=[VM] * len(operands) + [pl.BlockSpec(memory_space=pl.ANY)] * len(weights),
        out_specs=VM,
        scratch_shapes=[pltpu.VMEM(w.shape, w.dtype) for w in weights]
        + [
            dma((len(weights),)),
            pltpu.VMEM((columns // 128, HALF * WIN, 128), F32),
            pltpu.VMEM((lanes, WIN, 40, 128), BF16),
            pltpu.VMEM((lanes, WIN + 2, 40, 128), BF16),
            pltpu.VMEM((480, channels), F32),
            pltpu.VMEM((480, channels), BF16),
            pltpu.VMEM((512, channels), F32),
            pltpu.VMEM((WIN, 256), F32),
            pltpu.VMEM((512, 128), F32),
            pltpu.VMEM((512, 128), F32),
            pltpu.VMEM((channels // 128, 128, 128), F32),
            pltpu.VMEM((WIN, 4, 16, channels), BF16),
            pltpu.VMEM((WIN, 4, 16, channels), BF16),
            pltpu.VMEM((channels // 128, 512, 128), F32),
            pltpu.VMEM((WIN, lanes, 4, WIN, 128), BF16),
            pltpu.VMEM((WIN, lanes, 4, WIN, 128), BF16),
            pltpu.VMEM((columns, 128), F32),
            dma((4, lanes)), dma((4, lanes)), dma,
            dma((4, WIN)), dma((4, WIN)), dma((4,)),
            dma((4, WIN, lanes)), dma((4, WIN, lanes)), dma((4,)),
        ],
        compiler_params=pltpu.CompilerParams(
            collective_id=1, has_side_effects=True, vmem_limit_bytes=LIMIT
        ),
        name="maxvit",
    )(*operands, *weights)


def solution(mesh):
    in_specs = (P("ch", "rows", None),) + (P(),) * 15
    return jax.shard_map(
        shards, mesh=mesh, in_specs=in_specs, out_specs=P("ch", "rows", None), check_vma=False
    )
```
